32 devices in a mesh: dp: 4 (over y, x), seg: 8 (over z, core).
Axes of the slice: x: 2, y: 2, z: 4, core: 2. Of those that a mesh axis runs over, the one named last changes fastest.
Arguments:
- tokens: bfloat16 [128, 128, 768], P(('dp', 'seg')), may hold values from -6 to 6
- doc_counts: int32 [4, 6], replicated, may hold values from 1 to 24, 32 in all within a row
- pad_mask: int32 [4, 32], replicated, may hold values 0 or 1
- attn_in: bfloat16 [768, 2304], replicated, may hold values from -0.21875 to 0.21875
- attn_proj: bfloat16 [768, 768], replicated, may hold values from -0.625 to 0.625
- norm_attn: float32 [768], replicated, may hold values from 0.5 to 1.5
- ffn_up: bfloat16 [768, 3072], replicated, may hold values from -0.21875 to 0.21875
- ffn_down: bfloat16 [3072, 768], replicated, may hold values from -0.109375 to 0.109375
- norm_ffn: float32 [768], replicated, may hold values from 0.5 to 1.5
- segment_embed: float32 [32, 768], replicated, may hold values from -3 to 3
- cross_in: bfloat16 [768, 2304], replicated, may hold values from -0.21875 to 0.21875
- cross_proj: bfloat16 [768, 768], replicated, may hold values from -0.4375 to 0.4375
- cross_norm_attn: float32 [768], replicated, may hold values from 0.5 to 1.5
- cross_up: bfloat16 [768, 3072], replicated, may hold values from -0.21875 to 0.21875
- cross_down: bfloat16 [3072, 768], replicated, may hold values from -0.109375 to 0.109375
- cross_norm_ffn: float32 [768], replicated, may hold values from 0.5 to 1.5
- cotangent: bfloat16 [128, 128, 768], P(('dp', 'seg')), may hold values from -6 to 6
Outputs:
- output: bfloat16 [128, 128, 768], P(('dp', 'seg'))
- token_grad: bfloat16 [128, 128, 768], P(('dp', 'seg'))
- grad_attn_in: float32 [768, 2304], P('seg', 'dp')
- grad_attn_proj: float32 [768, 768], P('seg', 'dp')
- grad_norm_attn: float32 [768], P('seg')
- grad_ffn_up: float32 [768, 3072], P('seg', 'dp')
- grad_ffn_down: float32 [3072, 768], P('seg', 'dp')
- grad_norm_ffn: float32 [768], P('seg')
- grad_segment_embed: float32 [32, 768], P('dp', 'seg')
- grad_cross_in: float32 [768, 2304], P('seg', 'dp')
- grad_cross_proj: float32 [768, 768], P('seg', 'dp')
- grad_cross_norm_attn: float32 [768], P('seg')
- grad_cross_up: float32 [768, 3072], P('seg', 'dp')
- grad_cross_down: float32 [3072, 768], P('seg', 'dp')
- grad_cross_norm_ffn: float32 [768], P('seg')
The draws below stay inside these ranges and needn't reach their ends.
Inputs may be any that keep to these rules, and one draw needn't show every extreme that they name: `doc_counts`: the 6 document lengths of each slot sum to 32, and each slot has one of exactly 24 segments. `pad_mask`: 1 marks a padding segment.
All inputs are finite; a program needn't handle non-finite values.
Results may differ from the reference program's by a relative error of at most 0.023.
Values may be sent and summed in bfloat16 or wider, within the bound.
A program may use at most 192 MiB of HBM per device.

```python
import math
import jax
import jax.numpy as jnp
import numpy as np
from jax import lax

D = 768
H = 12
HD = 64
FF = 3072
SEG = 128
SLOT_SEGS = 32
SEG_DEV = 4
DOCS = 6
LONGEST = 24
SLOTS = 4
SEGS = 128
N_DP = 4
N_SEG = 8


def place_ends(values, key, low, largest):
    spot = [jax.random.randint(jax.random.fold_in(key, axis), (), 0, length) for axis, length in enumerate(values.shape)]
    main_axis = values.shape.index(max(values.shape))
    beside = spot[:main_axis] + [(spot[main_axis] + 1) % values.shape[main_axis]] + spot[main_axis + 1:]
    return values.at[tuple(spot)].set(low).at[tuple(beside)].set(largest)


def block_scale(stream_key, dims, pieces, least, high):
    gain, own = 1.0, jax.random.fold_in(stream_key, 6)
    for dim, blocks in pieces:
        steps = jnp.exp(jax.random.uniform(jax.random.fold_in(own, dim), (blocks,), jnp.float32, least / len(pieces), high / len(pieces)))
        gain = gain * jnp.repeat(steps, dims[dim] // blocks).reshape([-1 if axis == dim else 1 for axis in range(len(dims))])
    return gain


def length_profile(amount, total, bound, skew):
    weights = [(1 << 20) // math.isqrt(standing ** skew) + 1 for standing in range(2, amount + 1)]
    rest, given = total - bound - (amount - 1), [1] * (amount - 1)
    while rest > 0:
        candidates = [i for i in range(amount - 1) if given[i] < bound]
        whole, remaining = sum([weights[i] for i in candidates]), rest
        for i in candidates:
            more = min(bound - given[i], max(1, remaining * weights[i] // whole), rest)
            given[i] = given[i] + more
            rest = rest - more
    return np.array([bound] + given)


def ragged(own_key, amount, total, limit, skew):
    if amount == 2:
        one = jax.random.randint(own_key, (), max(1, total - limit), min(limit, total - 1) + 1)
        return jnp.stack([one, total - one])
    sizes = jnp.asarray(length_profile(amount, total, limit, skew), jnp.int32)
    twos = (amount - 1) // 2
    donor, receiver = sizes[1:1 + 2 * twos:2], sizes[2:2 + 2 * twos:2]
    slack = jnp.minimum(donor - 1, limit - receiver)
    shifted = jax.random.randint(jax.random.fold_in(own_key, 1), (twos,), 0, 1 << 20) % (slack + 1)
    sizes = sizes.at[1:1 + 2 * twos:2].set(donor - shifted).at[2:2 + 2 * twos:2].set(receiver + shifted)
    return sizes[jax.random.permutation(jax.random.fold_in(own_key, 2), amount)]


def gaussian(stream_key, dims, width, bound, pieces=(), kind=jnp.bfloat16):
    drawn = width * jax.random.normal(stream_key, dims, jnp.float32)
    if pieces:
        drawn = drawn * block_scale(stream_key, dims, pieces, -0.22, 0.18)
    return jnp.clip(drawn, -bound, bound).astype(kind)


def setup_inputs(seed: int = 0) -> dict:
    streams_of = jax.random.split(jax.random.key(seed), 18)
    tokens = gaussian(streams_of[0], (SEGS, SEG, D), 1.0, 6.0, ((0, 32),))
    doc_counts = jax.vmap(lambda own: ragged(own, DOCS, SLOT_SEGS, LONGEST, 2))(jax.random.split(streams_of[1], SLOTS)).reshape((SLOTS, DOCS)).astype(jnp.int32)
    pad_mask = place_ends((jax.random.randint(streams_of[2], (SLOTS, SLOT_SEGS), 0, 4) < 1).astype(jnp.int32), jax.random.fold_in(streams_of[2], 1), 0, 1)
    attn_in = gaussian(streams_of[3], (D, 3 * D), D ** -0.5, 0.21875)
    attn_proj = gaussian(streams_of[4], (D, D), (D // 8) ** -0.5, 0.625)
    norm_attn = jnp.clip(1.0 + 0.1 * jax.random.normal(streams_of[5], (D,), jnp.float32), 0.5, 1.5)
    ffn_up = gaussian(streams_of[6], (D, FF), D ** -0.5, 0.21875)
    ffn_down = gaussian(streams_of[7], (FF, D), FF ** -0.5, 0.109375)
    norm_ffn = jnp.clip(1.0 + 0.1 * jax.random.normal(streams_of[8], (D,), jnp.float32), 0.5, 1.5)
    segment_embed = gaussian(streams_of[9], (SLOT_SEGS, D), 0.5, 3.0, (), jnp.float32)
    cross_in = gaussian(streams_of[10], (D, 3 * D), D ** -0.5, 0.21875)
    cross_proj = gaussian(streams_of[11], (D, D), (D // 4) ** -0.5, 0.4375)
    cross_norm_attn = jnp.clip(1.0 + 0.1 * jax.random.normal(streams_of[12], (D,), jnp.float32), 0.5, 1.5)
    cross_up = gaussian(streams_of[13], (D, FF), D ** -0.5, 0.21875)
    cross_down = gaussian(streams_of[14], (FF, D), FF ** -0.5, 0.109375)
    cross_norm_ffn = jnp.clip(1.0 + 0.1 * jax.random.normal(streams_of[15], (D,), jnp.float32), 0.5, 1.5)
    cotangent = gaussian(streams_of[16], (SEGS, SEG, D), 1.0, 6.0, ((0, 32),))
    return dict(tokens=tokens, doc_counts=doc_counts, pad_mask=pad_mask, attn_in=attn_in, attn_proj=attn_proj, norm_attn=norm_attn, ffn_up=ffn_up, ffn_down=ffn_down, norm_ffn=norm_ffn, segment_embed=segment_embed, cross_in=cross_in, cross_proj=cross_proj, cross_norm_attn=cross_norm_attn, cross_up=cross_up, cross_down=cross_down, cross_norm_ffn=cross_norm_ffn, cotangent=cotangent)


EPSILON = 1e-05
MASKED = -1e+30

@jax.custom_vjp
def low(v):
    return lax.optimization_barrier(v.astype(jnp.bfloat16)).astype(jnp.float32)

@jax.custom_vjp
def low_back(v):
    return v

def low_keep(v):
    return (low(v), None)

def low_pass(kept, grad):
    return (grad,)

def back_keep(v):
    return (v, None)

def back_low(kept, grad):
    return (low(grad),)
low.defvjp(low_keep, low_pass)
low_back.defvjp(back_keep, back_low)

def rounded(value):
    return low(low_back(value))

def product(pattern, former, latter):
    return jnp.einsum(pattern, former, latter, precision=lax.Precision.HIGHEST)

def layer_norm(summed, gain_row):
    middle = summed - lax.optimization_barrier(jnp.mean(summed, -1, keepdims=True))
    return middle * lax.rsqrt(lax.optimization_barrier(jnp.mean(middle * middle, -1, keepdims=True)) + EPSILON) * gain_row

def block(residual, weights, allowed):
    attn_in, attn_proj, norm_attn, ffn_up, ffn_down, norm_ffn = weights
    batch_size, length, model_width = residual.shape
    packed = rounded(product('bld,de->ble', low(residual), attn_in))
    queries = packed[..., :model_width].reshape(batch_size, length, H, HD)
    key_heads = packed[..., model_width:2 * model_width].reshape(batch_size, length, H, HD)
    values = packed[..., 2 * model_width:].reshape(batch_size, length, H, HD)
    scores = low_back(product('bqhe,bkhe->bhqk', queries, key_heads) * HD ** (-0.5))
    if allowed is not None:
        scores = jnp.where(allowed, scores, MASKED)
    attn_probs = jax.nn.softmax(scores, axis=-1)
    attended = rounded(product('bhqk,bkhe->bqhe', low(attn_probs), values)).reshape(batch_size, length, model_width)
    first_norm = layer_norm(residual + low_back(product('bld,de->ble', attended, attn_proj)), norm_attn)
    pre_act = low_back(product('bld,df->blf', low(first_norm), ffn_up))
    hidden = low(jax.nn.gelu(pre_act, approximate=False))
    return layer_norm(first_norm + low_back(product('blf,fd->bld', hidden, ffn_down)), norm_ffn)

def slot_forward(segments, seg_weights, cross_weights, embed, embed_pick, allowed):
    seg_out = block(segments, seg_weights, None)
    cross_rows = seg_out[:, 0, :] + jnp.dot(embed_pick, embed, precision=lax.Precision.HIGHEST)
    cross_out = block(cross_rows[None], cross_weights, allowed[None, None])[0]
    return jnp.concatenate([cross_out[:, None, :], seg_out[:, 1:, :]], axis=1)

def layout():
    span_devs = SLOT_SEGS // SEG_DEV
    group_slots = N_SEG // span_devs
    half_count = SEG_DEV // 2
    table = np.zeros((N_DP * group_slots, SLOT_SEGS), np.int64)
    for group_index in range(N_DP):
        for device in range(N_SEG):
            for within in range(SEG_DEV):
                slot_index = (device // span_devs + within % half_count + group_slots // 2 * (within // half_count)) % group_slots
                position = within * span_devs + device % span_devs
                table[group_index * group_slots + slot_index, position] = (group_index * N_SEG + device) * SEG_DEV + within
    return table

def reference(tokens, doc_counts, pad_mask, attn_in, attn_proj, norm_attn, ffn_up, ffn_down, norm_ffn, segment_embed, cross_in, cross_proj, cross_norm_attn, cross_up, cross_down, cross_norm_ffn, cotangent):
    order = layout().reshape(-1)
    inverse = np.argsort(order)
    slot_tokens = tokens[order].astype(jnp.float32).reshape(SLOTS, SLOT_SEGS, SEG, D)
    slot_cots = cotangent[order].astype(jnp.float32).reshape(SLOTS, SLOT_SEGS, SEG, D)
    seg_weights = (attn_in.astype(jnp.float32), attn_proj.astype(jnp.float32), norm_attn, ffn_up.astype(jnp.float32), ffn_down.astype(jnp.float32), norm_ffn)
    cross_weights = (cross_in.astype(jnp.float32), cross_proj.astype(jnp.float32), cross_norm_attn, cross_up.astype(jnp.float32), cross_down.astype(jnp.float32), cross_norm_ffn)
    doc_ends = jnp.cumsum(doc_counts, axis=1)
    doc_starts = doc_ends - doc_counts
    places = jnp.arange(SLOT_SEGS, dtype=jnp.int32)
    document = lax.optimization_barrier(jnp.sum((doc_ends[:, None, :] <= places[None, :, None]).astype(jnp.int32), axis=2))
    is_first = jnp.any(doc_starts[:, None, :] == places[None, :, None], axis=2)
    doc_index = jnp.arange(DOCS, dtype=jnp.int32)
    doc_begin = lax.optimization_barrier(jnp.sum(jnp.where(doc_index[None, None, :] == document[:, :, None], doc_starts[:, None, :], 0), axis=2))
    doc_rank = places[None, :] - doc_begin
    embed_picks = (doc_rank[:, :, None] == places[None, None, :]).astype(jnp.float32)
    key_valid = (pad_mask == 0) | is_first
    masks = (document[:, :, None] == document[:, None, :]) & key_valid[:, None, :]

    def step(totals, item):
        segments, upstream, embed_pick, allowed = item

        def forward(seg_in, seg_w, cross_w, embed):
            return slot_forward(seg_in, seg_w, cross_w, embed, embed_pick, allowed)
        result, backward = jax.vjp(forward, segments, seg_weights, cross_weights, segment_embed)
        grad_tokens, grad_seg, grad_cross, grad_embed = backward(upstream)
        totals = jax.tree.map(jnp.add, totals, (grad_seg, grad_cross, grad_embed))
        return (totals, (result.astype(jnp.bfloat16), grad_tokens.astype(jnp.bfloat16)))
    zeros = jax.tree.map(jnp.zeros_like, (seg_weights, cross_weights, segment_embed))
    totals, (results, grads) = lax.scan(step, zeros, (slot_tokens, slot_cots, embed_picks, masks))
    output = results.reshape(SEGS, SEG, D)[inverse]
    token_grad = grads.reshape(SEGS, SEG, D)[inverse]
    grad_seg, grad_cross, grad_embed = totals
    return (output, token_grad, grad_seg[0], grad_seg[1], grad_seg[2], grad_seg[3], grad_seg[4], grad_seg[5], grad_embed, grad_cross[0], grad_cross[1], grad_cross[2], grad_cross[3], grad_cross[4], grad_cross[5])
```

```python
from functools import partial

import jax
import jax.numpy as jnp
import numpy as np
from jax import lax
from jax.sharding import PartitionSpec as P

H = 12
HD = 64
SLOT_SEGS = 32


EPSILON = 1e-05
MASKED = -1e30


def matmul(former, latter):
    return jnp.dot(former, latter, preferred_element_type=jnp.float32)


def exact_dot(former, latter):
    return jnp.dot(former, latter, precision=lax.Precision.HIGHEST)


def outer_sum(former, latter):
    return lax.dot_general(
        former, latter, (((0,), (0,)), ((), ())), preferred_element_type=jnp.float32
    )


def back_product(gradient, weight):
    return lax.dot_general(
        gradient, weight, (((1,), (1,)), ((), ())), preferred_element_type=jnp.float32
    )


def norm_forward(summed, gain_row):
    middle = summed - jnp.mean(summed, -1, keepdims=True)
    inverse = lax.rsqrt(jnp.mean(middle * middle, -1, keepdims=True) + EPSILON)
    unit_rows = middle * inverse
    return (unit_rows * gain_row, (unit_rows, inverse))


def norm_backward(state, gain_row, upstream):
    unit_rows, inverse = state
    scaled = upstream * gain_row
    centered = (
        scaled
        - jnp.mean(scaled, -1, keepdims=True)
        - unit_rows * jnp.mean(scaled * unit_rows, -1, keepdims=True)
    )
    return (inverse * centered, jnp.sum(upstream * unit_rows, 0))


def to_heads(columns, batch_size):
    return columns.reshape(batch_size, -1, H, HD)


def attend_forward(queries, key_heads, values, allowed):
    scores = jnp.einsum(
        "bqhe,bkhe->bhqk", queries, key_heads, preferred_element_type=jnp.float32
    ) * HD ** (-0.5)
    if allowed is not None:
        scores = jnp.where(allowed, scores, MASKED)
    attn_probs = jax.nn.softmax(scores, axis=-1)
    probs_low = attn_probs.astype(jnp.bfloat16)
    attended = jnp.einsum("bhqk,bkhe->bqhe", probs_low, values, preferred_element_type=jnp.float32)
    return (attn_probs, probs_low, attended.astype(jnp.bfloat16))


def score_grads(attn_probs, grad_att, values):
    grad_probs = jnp.einsum("bqhe,bkhe->bhqk", grad_att, values, preferred_element_type=jnp.float32)
    return (attn_probs * (grad_probs - jnp.sum(attn_probs * grad_probs, -1, keepdims=True))).astype(
        jnp.bfloat16
    )


def tail_forward(residual, attended, weights):
    attn_proj, norm_attn, ffn_up, ffn_down, norm_ffn = weights
    first_norm, first_state = norm_forward(residual + matmul(attended, attn_proj), norm_attn)
    first_low = first_norm.astype(jnp.bfloat16)
    pre_act = matmul(first_low, ffn_up)
    hidden = jax.nn.gelu(pre_act, approximate=False).astype(jnp.bfloat16)
    result, second_state = norm_forward(first_norm + matmul(hidden, ffn_down), norm_ffn)
    return (result, (attended, first_state, first_low, pre_act, hidden, second_state))


def tail_backward(state, weights, upstream):
    attn_proj, norm_attn, ffn_up, ffn_down, norm_ffn = weights
    attended, first_state, first_low, pre_act, hidden, second_state = state
    grad_second, grad_norm_ffn = norm_backward(second_state, norm_ffn, upstream)
    grad_out_low = grad_second.astype(jnp.bfloat16)
    grad_down = outer_sum(hidden, grad_out_low)
    spare, gelu_back = jax.vjp(partial(jax.nn.gelu, approximate=False), pre_act)
    grad_pre = gelu_back(back_product(grad_out_low, ffn_down))[0].astype(jnp.bfloat16)
    grad_up = outer_sum(first_low, grad_pre)
    grad_first = grad_second + back_product(grad_pre, ffn_up)
    grad_residual, grad_norm_attn = norm_backward(first_state, norm_attn, grad_first)
    grad_proj_out = grad_residual.astype(jnp.bfloat16)
    grad_proj = outer_sum(attended, grad_proj_out)
    grad_att = back_product(grad_proj_out, attn_proj).astype(jnp.bfloat16)
    grads = (grad_proj, grad_norm_attn, grad_up, grad_down, grad_norm_ffn)
    factors = (attended, grad_proj_out, first_low, grad_pre, hidden, grad_out_low)
    return (grad_residual, grad_att, grads, factors)


def segment_forward(token_rows, seg_count, weights):
    attn_in = weights[0]
    model_width = token_rows.shape[1]
    packed = matmul(token_rows, attn_in).astype(jnp.bfloat16)
    queries = to_heads(packed[:, :model_width], seg_count)
    key_heads = to_heads(packed[:, model_width : 2 * model_width], seg_count)
    values = to_heads(packed[:, 2 * model_width :], seg_count)
    attn_probs, probs_low, attended = attend_forward(queries, key_heads, values, None)
    result, state = tail_forward(
        token_rows.astype(jnp.float32), attended.reshape(token_rows.shape), weights[1:]
    )
    return (result, (queries, key_heads, values, attn_probs, probs_low, state))


def row_places(groups, members, seg_count):
    span_devs = SLOT_SEGS // seg_count
    group_slots = members // span_devs
    half_count = seg_count // 2
    row = np.arange(groups * members * seg_count)
    device, within = row // seg_count, row % seg_count
    group, member = device // members, device % members
    slot = group * group_slots + (
        member // span_devs + within % half_count + group_slots // 2 * (within // half_count)
    ) % group_slots
    return slot, within * span_devs + member % span_devs


def documents(doc_counts, pad_mask):
    doc_ends = jnp.cumsum(doc_counts, 1)
    doc_starts = doc_ends - doc_counts
    places = jnp.arange(pad_mask.shape[1], dtype=jnp.int32)
    document = jnp.sum((doc_ends[:, None, :] <= places[None, :, None]).astype(jnp.int32), 2)
    is_first = jnp.any(doc_starts[:, None, :] == places[None, :, None], 2)
    doc_index = jnp.arange(doc_counts.shape[1], dtype=jnp.int32)
    doc_begin = jnp.sum(
        jnp.where(doc_index[None, None] == document[:, :, None], doc_starts[:, None, :], 0), 2
    )
    return document, places[None] - doc_begin, (pad_mask == 0) | is_first


def cross_section(base, cot_rows, embed_pick, allowed, segment_embed, weights):
    cross_in = weights[0]
    tail_weights = weights[1:]
    rows, width = base.shape
    slots = rows // SLOT_SEGS
    cross_input = base + exact_dot(embed_pick, segment_embed)
    cross_low = cross_input.astype(jnp.bfloat16)
    packed = matmul(cross_low, cross_in).astype(jnp.bfloat16)
    queries = to_heads(packed[:, :width], slots)
    keys = to_heads(packed[:, width : 2 * width], slots)
    values = to_heads(packed[:, 2 * width :], slots)
    probs, probs_low, attended = attend_forward(queries, keys, values, allowed)
    result, state = tail_forward(cross_input, attended.reshape(rows, width), tail_weights)
    grad_in, grad_att, tail_grads, factors = tail_backward_factors(state, tail_weights, cot_rows)
    grad_packed = attend_backward(probs, probs_low, queries, keys, values, to_heads(grad_att, slots), rows)
    grad_input = grad_in + back_product(grad_packed, cross_in)
    return result, grad_input, (cross_low, grad_packed) + factors, tail_grads


def attend_backward(probs, probs_low, queries, keys, values, grad_att, rows):
    scores_grad = score_grads(probs, grad_att, values)
    grad_query = jnp.einsum("bhqk,bkhe->bqhe", scores_grad, keys, preferred_element_type=jnp.float32) * HD ** (-0.5)
    grad_key = jnp.einsum("bhqk,bqhe->bkhe", scores_grad, queries, preferred_element_type=jnp.float32) * HD ** (-0.5)
    grad_value = jnp.einsum("bhqk,bqhe->bkhe", probs_low, grad_att, preferred_element_type=jnp.float32)
    return jnp.concatenate([g.reshape(rows, H * HD) for g in (grad_query, grad_key, grad_value)], 1).astype(jnp.bfloat16)


def tail_backward_factors(state, weights, upstream):
    attn_proj, norm_attn, ffn_up, ffn_down, norm_ffn = weights
    attended, first_state, first_low, pre_act, hidden, second_state = state
    grad_second, grad_norm_ffn = norm_backward(second_state, norm_ffn, upstream)
    grad_out_low = grad_second.astype(jnp.bfloat16)
    spare, gelu_back = jax.vjp(partial(jax.nn.gelu, approximate=False), pre_act)
    grad_pre = gelu_back(back_product(grad_out_low, ffn_down))[0].astype(jnp.bfloat16)
    grad_first = grad_second + back_product(grad_pre, ffn_up)
    grad_residual, grad_norm_attn = norm_backward(first_state, norm_attn, grad_first)
    grad_proj_out = grad_residual.astype(jnp.bfloat16)
    grad_att = back_product(grad_proj_out, attn_proj).astype(jnp.bfloat16)
    factors = (attended, grad_proj_out, first_low, grad_pre, hidden, grad_out_low)
    return grad_residual, grad_att, (grad_norm_attn, grad_norm_ffn), factors


def reduce_weights(grads, groups, members):
    parts = [lax.psum_scatter(g.astype(jnp.bfloat16), "seg", scatter_dimension=0, tiled=True) for g in grads]
    flat = [p.reshape(p.shape[0], groups, -1).transpose(1, 0, 2).reshape(groups, -1) for p in parts]
    joined = lax.psum_scatter(jnp.concatenate(flat, 1), "dp", scatter_dimension=0, tiled=True)[0].astype(jnp.float32)
    outs, at = [], 0
    for p in parts:
        rows, columns = p.shape[0], p.shape[1] // groups
        outs.append(joined[at : at + rows * columns].reshape(rows, columns))
        at += rows * columns
    return outs


def on_device(
    tokens, doc_counts, pad_mask, attn_in, attn_proj, norm_attn, ffn_up, ffn_down, norm_ffn,
    segment_embed, cross_in, cross_proj, cross_norm_attn, cross_up, cross_down, cross_norm_ffn,
    cotangent,
):
    seg_count, seg_length, width = tokens.shape
    rows = seg_count * seg_length
    members, groups = lax.axis_size("seg"), lax.axis_size("dp")
    member, group = lax.axis_index("seg"), lax.axis_index("dp")
    device = group * members + member
    token_rows = tokens.reshape(rows, width)
    seg_weights = (attn_in, attn_proj, norm_attn, ffn_up, ffn_down, norm_ffn)
    cross_weights = (cross_in, cross_proj, cross_norm_attn, cross_up, cross_down, cross_norm_ffn)

    slot_of, place_of = row_places(groups, members, seg_count)
    order = np.argsort(slot_of * SLOT_SEGS + place_of)
    slots = pad_mask.shape[0]
    document, rank, key_ok = documents(doc_counts, pad_mask)
    allowed = (document[:, :, None] == document[:, None, :]) & key_ok[:, None, :]
    embed_pick = (
        rank.reshape(-1)[:, None] == jnp.arange(segment_embed.shape[0], dtype=jnp.int32)[None]
    ).astype(jnp.float32)

    cot_first = lax.all_gather(cotangent[:, 0, :], ("dp", "seg"), axis=0, tiled=True)[order]
    seg_result, seg_state = segment_forward(token_rows, seg_count, seg_weights)
    seg_cube = seg_result.reshape(seg_count, seg_length, width)
    base = lax.all_gather(seg_cube[:, 0, :], ("dp", "seg"), axis=0, tiled=True)[order]
    cross_result, cross_grad, factors, cross_gains = cross_section(
        base, cot_first.astype(jnp.float32), embed_pick, allowed[:, None], segment_embed, cross_weights
    )
    back = np.argsort(order)
    own = lambda a: lax.dynamic_slice_in_dim(a[back], device * seg_count, seg_count, 0)
    output = jnp.concatenate(
        [own(cross_result.astype(jnp.bfloat16))[:, None, :], seg_cube[:, 1:, :].astype(jnp.bfloat16)], 1
    )

    def share(left, right):
        r, c = left.shape[1] // members, right.shape[1] // groups
        return outer_sum(
            lax.dynamic_slice_in_dim(left, member * r, r, 1), lax.dynamic_slice_in_dim(right, group * c, c, 1)
        )

    cross_low, cross_packed, cross_att, cross_proj_out, cross_first, cross_pre, cross_hidden, cross_out = factors
    grad_cross_in = share(cross_low, cross_packed)
    grad_cross_proj = share(cross_att, cross_proj_out)
    grad_cross_up = share(cross_first, cross_pre)
    grad_cross_down = share(cross_hidden, cross_out)
    er, ec = segment_embed.shape[0] // groups, width // members
    grad_embed = lax.dot_general(
        lax.dynamic_slice_in_dim(embed_pick, group * er, er, 1),
        lax.dynamic_slice_in_dim(cross_grad, member * ec, ec, 1),
        (((0,), (0,)), ((), ())), precision=lax.Precision.HIGHEST,
    )
    piece = lambda g: lax.dynamic_slice_in_dim(g, member * ec, ec, 0)

    upstream = cotangent.astype(jnp.float32)
    seg_upstream = jnp.concatenate([own(cross_grad)[:, None, :], upstream[:, 1:, :]], 1).reshape(rows, width)
    queries, key_heads, values, attn_probs, probs_low, tail_state = seg_state
    grad_residual, grad_att, seg_tail_grads, spare = tail_backward(tail_state, seg_weights[1:], seg_upstream)
    grad_packed = attend_backward(
        attn_probs, probs_low, queries, key_heads, values, to_heads(grad_att, seg_count), rows
    )
    grad_attn_in = outer_sum(token_rows, grad_packed)
    token_grad = (grad_residual + back_product(grad_packed, attn_in)).astype(jnp.bfloat16).reshape(tokens.shape)
    grad_attn_proj, grad_norm_attn, grad_ffn_up, grad_ffn_down, grad_norm_ffn = seg_tail_grads
    total_in, total_proj, total_up, total_down = reduce_weights(
        (grad_attn_in, grad_attn_proj, grad_ffn_up, grad_ffn_down), groups, members
    )
    gains = lax.psum(jnp.concatenate([grad_norm_attn, grad_norm_ffn]), ("dp", "seg"))
    return (
        output, token_grad, total_in, total_proj, piece(gains[:width]), total_up, total_down,
        piece(gains[width:]), grad_embed, grad_cross_in, grad_cross_proj, piece(cross_gains[0]),
        grad_cross_up, grad_cross_down, piece(cross_gains[1]),
    )


def solution(mesh):
    placed = (
        P(("dp", "seg"), None, None),
        P(),
        P(),
        P(),
        P(),
        P(),
        P(),
        P(),
        P(),
        P(),
        P(),
        P(),
        P(),
        P(),
        P(),
        P(),
        P(("dp", "seg"), None, None),
    )
    return jax.shard_map(
        on_device,
        mesh=mesh,
        in_specs=placed,
        out_specs=(
            P(("dp", "seg"), None, None),
            P(("dp", "seg"), None, None),
            P("seg", "dp"),
            P("seg", "dp"),
            P("seg"),
            P("seg", "dp"),
            P("seg", "dp"),
            P("seg"),
            P("dp", "seg"),
            P("seg", "dp"),
            P("seg", "dp"),
            P("seg"),
            P("seg", "dp"),
            P("seg", "dp"),
            P("seg"),
        ),
        check_vma=False,
    )
```

```python
from functools import partial

import jax
import jax.numpy as jnp
import numpy as np
from jax.experimental import pallas as pl
from jax.experimental.pallas import tpu as pltpu
from jax import lax
from jax.sharding import PartitionSpec as P

H = 12
HD = 64
SLOT_SEGS = 32


EPSILON = 1e-05
MASKED = -1e30


def matmul(former, latter):
    return jnp.dot(former, latter, preferred_element_type=jnp.float32)


def exact_dot(former, latter):
    return jnp.dot(former, latter, precision=lax.Precision.HIGHEST)


def outer_sum(former, latter):
    return lax.dot_general(
        former, latter, (((0,), (0,)), ((), ())), preferred_element_type=jnp.float32
    )


def back_product(gradient, weight):
    return lax.dot_general(
        gradient, weight, (((1,), (1,)), ((), ())), preferred_element_type=jnp.float32
    )


def norm_forward(summed, gain_row):
    middle = summed - jnp.mean(summed, -1, keepdims=True)
    inverse = lax.rsqrt(jnp.mean(middle * middle, -1, keepdims=True) + EPSILON)
    unit_rows = middle * inverse
    return (unit_rows * gain_row, (unit_rows, inverse))


def norm_backward(state, gain_row, upstream):
    unit_rows, inverse = state
    scaled = upstream * gain_row
    centered = (
        scaled
        - jnp.mean(scaled, -1, keepdims=True)
        - unit_rows * jnp.mean(scaled * unit_rows, -1, keepdims=True)
    )
    return (inverse * centered, jnp.sum(upstream * unit_rows, 0))


def to_heads(columns, batch_size):
    return columns.reshape(batch_size, -1, H, HD)


def attend_forward(queries, key_heads, values, allowed):
    scores = jnp.einsum(
        "bqhe,bkhe->bhqk", queries, key_heads, preferred_element_type=jnp.float32
    ) * HD ** (-0.5)
    if allowed is not None:
        scores = jnp.where(allowed, scores, MASKED)
    attn_probs = jax.nn.softmax(scores, axis=-1)
    probs_low = attn_probs.astype(jnp.bfloat16)
    attended = jnp.einsum("bhqk,bkhe->bqhe", probs_low, values, preferred_element_type=jnp.float32)
    return (attn_probs, probs_low, attended.astype(jnp.bfloat16))


def score_grads(attn_probs, grad_att, values):
    grad_probs = jnp.einsum("bqhe,bkhe->bhqk", grad_att, values, preferred_element_type=jnp.float32)
    return (attn_probs * (grad_probs - jnp.sum(attn_probs * grad_probs, -1, keepdims=True))).astype(
        jnp.bfloat16
    )


def tail_forward(residual, attended, weights):
    attn_proj, norm_attn, ffn_up, ffn_down, norm_ffn = weights
    first_norm, first_state = norm_forward(residual + matmul(attended, attn_proj), norm_attn)
    first_low = first_norm.astype(jnp.bfloat16)
    pre_act = matmul(first_low, ffn_up)
    hidden = jax.nn.gelu(pre_act, approximate=False).astype(jnp.bfloat16)
    result, second_state = norm_forward(first_norm + matmul(hidden, ffn_down), norm_ffn)
    return (result, (attended, first_state, first_low, pre_act, hidden, second_state))


def tail_backward(state, weights, upstream):
    attn_proj, norm_attn, ffn_up, ffn_down, norm_ffn = weights
    attended, first_state, first_low, pre_act, hidden, second_state = state
    grad_second, grad_norm_ffn = norm_backward(second_state, norm_ffn, upstream)
    grad_out_low = grad_second.astype(jnp.bfloat16)
    grad_down = outer_sum(hidden, grad_out_low)
    spare, gelu_back = jax.vjp(partial(jax.nn.gelu, approximate=False), pre_act)
    grad_pre = gelu_back(back_product(grad_out_low, ffn_down))[0].astype(jnp.bfloat16)
    grad_up = outer_sum(first_low, grad_pre)
    grad_first = grad_second + back_product(grad_pre, ffn_up)
    grad_residual, grad_norm_attn = norm_backward(first_state, norm_attn, grad_first)
    grad_proj_out = grad_residual.astype(jnp.bfloat16)
    grad_proj = outer_sum(attended, grad_proj_out)
    grad_att = back_product(grad_proj_out, attn_proj).astype(jnp.bfloat16)
    grads = (grad_proj, grad_norm_attn, grad_up, grad_down, grad_norm_ffn)
    factors = (attended, grad_proj_out, first_low, grad_pre, hidden, grad_out_low)
    return (grad_residual, grad_att, grads, factors)


def segment_forward(token_rows, seg_count, weights):
    attn_in = weights[0]
    model_width = token_rows.shape[1]
    packed = matmul(token_rows, attn_in).astype(jnp.bfloat16)
    queries = to_heads(packed[:, :model_width], seg_count)
    key_heads = to_heads(packed[:, model_width : 2 * model_width], seg_count)
    values = to_heads(packed[:, 2 * model_width :], seg_count)
    attn_probs, probs_low, attended = attend_forward(queries, key_heads, values, None)
    result, state = tail_forward(
        token_rows.astype(jnp.float32), attended.reshape(token_rows.shape), weights[1:]
    )
    return (result, (queries, key_heads, values, attn_probs, probs_low, state))


def row_places(groups, members, seg_count):
    span_devs = SLOT_SEGS // seg_count
    group_slots = members // span_devs
    half_count = seg_count // 2
    row = np.arange(groups * members * seg_count)
    device, within = row // seg_count, row % seg_count
    group, member = device // members, device % members
    slot = group * group_slots + (
        member // span_devs + within % half_count + group_slots // 2 * (within // half_count)
    ) % group_slots
    return slot, within * span_devs + member % span_devs


def documents(doc_counts, pad_mask):
    doc_ends = jnp.cumsum(doc_counts, 1)
    doc_starts = doc_ends - doc_counts
    places = jnp.arange(pad_mask.shape[1], dtype=jnp.int32)
    document = jnp.sum((doc_ends[:, None, :] <= places[None, :, None]).astype(jnp.int32), 2)
    is_first = jnp.any(doc_starts[:, None, :] == places[None, :, None], 2)
    doc_index = jnp.arange(doc_counts.shape[1], dtype=jnp.int32)
    doc_begin = jnp.sum(
        jnp.where(doc_index[None, None] == document[:, :, None], doc_starts[:, None, :], 0), 2
    )
    return document, places[None] - doc_begin, (pad_mask == 0) | is_first


def cross_section(base, cot_rows, embed_pick, allowed, segment_embed, weights):
    cross_in = weights[0]
    tail_weights = weights[1:]
    rows, width = base.shape
    slots = rows // SLOT_SEGS
    cross_input = base + exact_dot(embed_pick, segment_embed)
    cross_low = cross_input.astype(jnp.bfloat16)
    packed = matmul(cross_low, cross_in).astype(jnp.bfloat16)
    queries = to_heads(packed[:, :width], slots)
    keys = to_heads(packed[:, width : 2 * width], slots)
    values = to_heads(packed[:, 2 * width :], slots)
    probs, probs_low, attended = attend_forward(queries, keys, values, allowed)
    result, state = tail_forward(cross_input, attended.reshape(rows, width), tail_weights)
    grad_in, grad_att, tail_grads, factors = tail_backward_factors(state, tail_weights, cot_rows)
    grad_packed = attend_backward(probs, probs_low, queries, keys, values, to_heads(grad_att, slots), rows)
    grad_input = grad_in + back_product(grad_packed, cross_in)
    return result, grad_input, (cross_low, grad_packed) + factors, tail_grads


def attend_backward(probs, probs_low, queries, keys, values, grad_att, rows):
    scores_grad = score_grads(probs, grad_att, values)
    grad_query = jnp.einsum("bhqk,bkhe->bqhe", scores_grad, keys, preferred_element_type=jnp.float32) * HD ** (-0.5)
    grad_key = jnp.einsum("bhqk,bqhe->bkhe", scores_grad, queries, preferred_element_type=jnp.float32) * HD ** (-0.5)
    grad_value = jnp.einsum("bhqk,bqhe->bkhe", probs_low, grad_att, preferred_element_type=jnp.float32)
    return jnp.concatenate([g.reshape(rows, H * HD) for g in (grad_query, grad_key, grad_value)], 1).astype(jnp.bfloat16)


def tail_backward_factors(state, weights, upstream):
    attn_proj, norm_attn, ffn_up, ffn_down, norm_ffn = weights
    attended, first_state, first_low, pre_act, hidden, second_state = state
    grad_second, grad_norm_ffn = norm_backward(second_state, norm_ffn, upstream)
    grad_out_low = grad_second.astype(jnp.bfloat16)
    spare, gelu_back = jax.vjp(partial(jax.nn.gelu, approximate=False), pre_act)
    grad_pre = gelu_back(back_product(grad_out_low, ffn_down))[0].astype(jnp.bfloat16)
    grad_first = grad_second + back_product(grad_pre, ffn_up)
    grad_residual, grad_norm_attn = norm_backward(first_state, norm_attn, grad_first)
    grad_proj_out = grad_residual.astype(jnp.bfloat16)
    grad_att = back_product(grad_proj_out, attn_proj).astype(jnp.bfloat16)
    factors = (attended, grad_proj_out, first_low, grad_pre, hidden, grad_out_low)
    return grad_residual, grad_att, (grad_norm_attn, grad_norm_ffn), factors


def reduce_weights(grads, groups, members):
    parts = [lax.psum_scatter(g.astype(jnp.bfloat16), "seg", scatter_dimension=0, tiled=True) for g in grads]
    flat = [p.reshape(p.shape[0], groups, -1).transpose(1, 0, 2).reshape(groups, -1) for p in parts]
    joined = lax.psum_scatter(jnp.concatenate(flat, 1), "dp", scatter_dimension=0, tiled=True)[0].astype(jnp.float32)
    outs, at = [], 0
    for p in parts:
        rows, columns = p.shape[0], p.shape[1] // groups
        outs.append(joined[at : at + rows * columns].reshape(rows, columns))
        at += rows * columns
    return outs


def any_mesh(
    tokens, doc_counts, pad_mask, attn_in, attn_proj, norm_attn, ffn_up, ffn_down, norm_ffn,
    segment_embed, cross_in, cross_proj, cross_norm_attn, cross_up, cross_down, cross_norm_ffn,
    cotangent,
):
    seg_count, seg_length, width = tokens.shape
    rows = seg_count * seg_length
    members, groups = lax.axis_size("seg"), lax.axis_size("dp")
    member, group = lax.axis_index("seg"), lax.axis_index("dp")
    device = group * members + member
    token_rows = tokens.reshape(rows, width)
    seg_weights = (attn_in, attn_proj, norm_attn, ffn_up, ffn_down, norm_ffn)
    cross_weights = (cross_in, cross_proj, cross_norm_attn, cross_up, cross_down, cross_norm_ffn)

    slot_of, place_of = row_places(groups, members, seg_count)
    order = np.argsort(slot_of * SLOT_SEGS + place_of)
    slots = pad_mask.shape[0]
    document, rank, key_ok = documents(doc_counts, pad_mask)
    allowed = (document[:, :, None] == document[:, None, :]) & key_ok[:, None, :]
    embed_pick = (
        rank.reshape(-1)[:, None] == jnp.arange(segment_embed.shape[0], dtype=jnp.int32)[None]
    ).astype(jnp.float32)

    cot_first = lax.all_gather(cotangent[:, 0, :], ("dp", "seg"), axis=0, tiled=True)[order]
    seg_result, seg_state = segment_forward(token_rows, seg_count, seg_weights)
    seg_cube = seg_result.reshape(seg_count, seg_length, width)
    base = lax.all_gather(seg_cube[:, 0, :], ("dp", "seg"), axis=0, tiled=True)[order]
    cross_result, cross_grad, factors, cross_gains = cross_section(
        base, cot_first.astype(jnp.float32), embed_pick, allowed[:, None], segment_embed, cross_weights
    )
    back = np.argsort(order)
    own = lambda a: lax.dynamic_slice_in_dim(a[back], device * seg_count, seg_count, 0)
    output = jnp.concatenate(
        [own(cross_result.astype(jnp.bfloat16))[:, None, :], seg_cube[:, 1:, :].astype(jnp.bfloat16)], 1
    )

    def share(left, right):
        r, c = left.shape[1] // members, right.shape[1] // groups
        return outer_sum(
            lax.dynamic_slice_in_dim(left, member * r, r, 1), lax.dynamic_slice_in_dim(right, group * c, c, 1)
        )

    cross_low, cross_packed, cross_att, cross_proj_out, cross_first, cross_pre, cross_hidden, cross_out = factors
    grad_cross_in = share(cross_low, cross_packed)
    grad_cross_proj = share(cross_att, cross_proj_out)
    grad_cross_up = share(cross_first, cross_pre)
    grad_cross_down = share(cross_hidden, cross_out)
    er, ec = segment_embed.shape[0] // groups, width // members
    grad_embed = lax.dot_general(
        lax.dynamic_slice_in_dim(embed_pick, group * er, er, 1),
        lax.dynamic_slice_in_dim(cross_grad, member * ec, ec, 1),
        (((0,), (0,)), ((), ())), precision=lax.Precision.HIGHEST,
    )
    piece = lambda g: lax.dynamic_slice_in_dim(g, member * ec, ec, 0)

    upstream = cotangent.astype(jnp.float32)
    seg_upstream = jnp.concatenate([own(cross_grad)[:, None, :], upstream[:, 1:, :]], 1).reshape(rows, width)
    queries, key_heads, values, attn_probs, probs_low, tail_state = seg_state
    grad_residual, grad_att, seg_tail_grads, spare = tail_backward(tail_state, seg_weights[1:], seg_upstream)
    grad_packed = attend_backward(
        attn_probs, probs_low, queries, key_heads, values, to_heads(grad_att, seg_count), rows
    )
    grad_attn_in = outer_sum(token_rows, grad_packed)
    token_grad = (grad_residual + back_product(grad_packed, attn_in)).astype(jnp.bfloat16).reshape(tokens.shape)
    grad_attn_proj, grad_norm_attn, grad_ffn_up, grad_ffn_down, grad_norm_ffn = seg_tail_grads
    total_in, total_proj, total_up, total_down = reduce_weights(
        (grad_attn_in, grad_attn_proj, grad_ffn_up, grad_ffn_down), groups, members
    )
    gains = lax.psum(jnp.concatenate([grad_norm_attn, grad_norm_ffn]), ("dp", "seg"))
    return (
        output, token_grad, total_in, total_proj, piece(gains[:width]), total_up, total_down,
        piece(gains[width:]), grad_embed, grad_cross_in, grad_cross_proj, piece(cross_gains[0]),
        grad_cross_up, grad_cross_down, piece(cross_gains[1]),
    )


BF16, F32 = jnp.bfloat16, jnp.float32
QUAD = 4 * HD
ERFC = (0.23192104, 0.16183046, 0.46825631, -0.37088501, 0.70913273, -0.20025555)

def nn(a, b): return jnp.dot(a, b, preferred_element_type=F32)
def nt(a, b): return lax.dot_general(a, b, (((1,), (1,)), ((), ())), preferred_element_type=F32)
def tn(a, b): return lax.dot_general(a, b, (((0,), (0,)), ((), ())), preferred_element_type=F32)

def gelu_pair(v):
    size = jnp.abs(v)
    t = 1.0 / (1.0 + (0.4 * 0.5 ** 0.5) * size)
    bell = jnp.exp(-0.5 * (v * v))
    poly = F32(0.5 * ERFC[5])
    for c in ERFC[4::-1]:
        poly = poly * t + F32(0.5 * c)
    tail = poly * t * bell
    cdf = jnp.where(v >= 0, 1.0 - tail, tail)
    scaled = v * cdf
    return scaled, cdf + v * (bell * F32((2 * np.pi) ** -0.5))

def mean(v): return jnp.mean(v, -1, keepdims=True)

def unit(total):
    middle = total - mean(total)
    inverse = lax.rsqrt(mean(middle * middle) + EPSILON)
    return middle * inverse, inverse

def lanes(start, size):
    return pl.ds(pl.multiple_of(start, 128), size)

def head_mask(rows):
    lane = lax.broadcasted_iota(jnp.int32, (rows, QUAD), 1)
    return [lane // HD == h for h in range(4)]

def stacked(v, masks):
    zero = jnp.zeros_like(v)
    return jnp.concatenate([jnp.where(m, v, zero) for m in masks], 0)

def picked(v, masks):
    n = v.shape[0] // 4
    out = v[3 * n :]
    for h in (2, 1, 0):
        out = jnp.where(masks[h], v[h * n : (h + 1) * n], out)
    return out

def forward_kernel(segs, x, w_in, w_proj, w_up, w_down, ga, gf,
                   qkv_o, probs_o, att_o, unit1_o, unit2_o, inv_o, hidden_o, slope_o, out_o, row_o,
                   win, wproj, wup, wdown, qkv, probs, att, unit1, unit2, inv, hidden, slope, out, acc, low, in_sem, out_sem):
    rows, width = x.shape
    length = rows // segs
    loads = [pltpu.make_async_copy(a, b, in_sem.at[k]) for k, (a, b) in enumerate(((w_in, win), (w_proj, wproj), (w_up, wup), (w_down, wdown)))]
    for load in loads: load.start()
    saves = []
    def save(a, b):
        copy = pltpu.make_async_copy(a, b, out_sem.at[len(saves)])
        copy.start(); saves.append(copy)
    loads[0].wait()
    def project(n, c):
        s = lanes(n * width, width)
        qkv[:, s] = nn(x[...], win[:, s]).astype(BF16)
        return c
    lax.fori_loop(0, 3, project, 0)
    save(qkv, qkv_o)
    masks = head_mask(length)
    def attend(n, c):
        seg, quad = n // 3, n % 3
        r = pl.ds(pl.multiple_of(seg * length, length), length)
        q = stacked(qkv[r, lanes(quad * QUAD, QUAD)], masks)
        scores = nt(q, qkv[r, lanes(width + quad * QUAD, QUAD)]) * HD ** -0.5
        e = jnp.exp(scores - jnp.max(scores, -1, keepdims=True))
        p = e / jnp.sum(e, -1, keepdims=True)
        probs[n] = p
        o = nn(p.astype(BF16), qkv[r, lanes(2 * width + quad * QUAD, QUAD)])
        att[r, lanes(quad * QUAD, QUAD)] = picked(o, masks).astype(BF16)
        return c
    lax.fori_loop(0, 3 * segs, attend, 0)
    save(probs, probs_o); save(att, att_o)
    loads[1].wait()
    acc[...] = nn(att[...], wproj[...])
    def first(n, c):
        r = pl.ds(pl.multiple_of(n * length, length), length)
        u, i = unit(x[r, :].astype(F32) + acc[r, :])
        unit1[r, :] = u
        inv[0, r, :] = jnp.broadcast_to(i, (length, 128))
        f = u * ga[...]
        acc[r, :] = f
        low[r, :] = f.astype(BF16)
        return c
    lax.fori_loop(0, segs, first, 0)
    save(unit1, unit1_o)
    loads[2].wait()
    tile = 512
    def up(n, c):
        s = lanes(n * tile, tile)
        h, g = gelu_pair(nn(low[...], wup[:, s]))
        hidden[:, s] = h.astype(BF16)
        slope[:, s] = g.astype(BF16)
        return c
    lax.fori_loop(0, wup.shape[1] // tile, up, 0)
    save(hidden, hidden_o); save(slope, slope_o)
    loads[3].wait()
    def down(n, c):
        s = lanes(n * QUAD, QUAD)
        acc[:, s] += nn(hidden[...], wdown[:, s])
        return c
    lax.fori_loop(0, width // QUAD, down, 0)
    def second(n, c):
        r = pl.ds(pl.multiple_of(n * length, length), length)
        u, i = unit(acc[r, :])
        unit2[r, :] = u
        inv[1, r, :] = jnp.broadcast_to(i, (length, 128))
        o = u * gf[...]
        out[r, :] = o.astype(BF16)
        row_o[pl.ds(n, 1), :] = o[:1]
        return c
    lax.fori_loop(0, segs, second, 0)
    save(unit2, unit2_o); save(inv, inv_o); save(out, out_o)
    for copy in saves: copy.wait()

ANY = pl.BlockSpec(memory_space=pl.ANY)
VM = pl.BlockSpec(memory_space=pltpu.VMEM)
def sds(*a): return jax.ShapeDtypeStruct(*a)

def forward(x, segs, weights):
    w_in, w_proj, ga, w_up, w_down, gf = weights
    rows, width = x.shape
    ff = w_up.shape[1]
    length = rows // segs
    saved = [((rows, 3 * width), BF16), ((3 * segs, 4 * length, length), F32), ((rows, width), BF16), ((rows, width), F32),
             ((rows, width), F32), ((2, rows, 128), F32), ((rows, ff), BF16), ((rows, ff), BF16), ((rows, width), BF16)]
    return pl.pallas_call(
        partial(forward_kernel, segs),
        out_shape=[sds(*s) for s in saved] + [sds((segs, width), F32)],
        in_specs=[VM, ANY, ANY, ANY, ANY, VM, VM],
        out_specs=[ANY] * 9 + [VM],
        scratch_shapes=[pltpu.VMEM(w.shape, BF16) for w in (w_in, w_proj, w_up, w_down)]
        + [pltpu.VMEM(*s) for s in saved]
        + [pltpu.VMEM((rows, width), F32), pltpu.VMEM((rows, width), BF16), pltpu.SemaphoreType.DMA((4,)), pltpu.SemaphoreType.DMA((9,))],
        compiler_params=pltpu.CompilerParams(vmem_limit_bytes=60 << 20),
        name="segment_forward",
    )(x, w_in, w_proj, w_up, w_down, ga.reshape(1, -1), gf.reshape(1, -1))

NC = 12
MESH = pl.DeviceIdType.MESH

def spots():
    dp, seg = lax.axis_index("dp"), lax.axis_index("seg")
    return dp // 2, dp % 2, seg // 2, seg % 2

def norm_back(u, i, up, gain):
    s = up * gain
    return i * (s - mean(s) - u * mean(s * u)), jnp.sum(up * u, 0, keepdims=True)

def backward_body(segs, x, cot, crossed, win, wproj, wup, wdown, ga, gf, qkv, probs, att, unit1, unit2, inv, hidden, slope,
                  low, dy, gains, g, ready, tick):
    rows, width = x.shape
    length = rows // segs
    ff = wup.shape[1]
    top = lax.broadcasted_iota(jnp.int32, (length, 1), 0) == 0

    def put(chunk, y, v, core_rows=96):
        v = v.astype(BF16)
        for j in range(8):
            z, core = j // 2, j % 2
            h, zz = z // 2, z % 2
            for half in range(2):
                part = v[j * 96 + half * 48 : j * 96 + half * 48 + 48]
                p, q = (half, y) if h == 0 else (y, half)
                g[chunk, core, h, p, q, zz] = part

    gains[...] = jnp.zeros_like(gains)
    def second(n, c):
        r = pl.ds(pl.multiple_of(n * length, length), length)
        up = jnp.where(top, crossed[pl.ds(n, 1), :], cot[r, :].astype(F32))
        d, gain = norm_back(unit2[r, :], inv[1, r, :1], up, gf[...])
        gains[1:2, :] += gain
        unit2[r, :] = d
        dy[r, :] = d.astype(BF16)
        low[r, :] = (unit1[r, :] * ga[...]).astype(BF16)
        return c
    ready("norms")
    lax.fori_loop(0, segs, second, 0)
    ready("hidden")
    def down_grad(j, c):
        v = tn(hidden[:, lanes(j * 384, 384)], dy[...]).astype(BF16)
        z, core = j // 2, j % 2
        h, zz = z // 2, z % 2
        for chunk in range(4):
            for half in range(2):
                for y in range(2):
                    part = v[chunk * 96 + half * 48 : chunk * 96 + half * 48 + 48, y * 384 : y * 384 + 384]
                    p = half * (1 - h) + y * h
                    q = y * (1 - h) + half * h
                    g[chunk, core, h, p, q, zz] = part
        return c
    lax.fori_loop(0, 8, down_grad, 0)
    tick("down")
    ready("slope")
    tile = 512
    def pre_grad(n, c):
        s = lanes(n * tile, tile)
        slope[:, s] = (nt(dy[...], wdown[pl.ds(pl.multiple_of(n * tile, tile), tile), :]) * slope[:, s].astype(F32)).astype(BF16)
        return c
    lax.fori_loop(0, ff // tile, pre_grad, 0)
    def up_grad(n, c):
        chunk, y = n // 2, n % 2
        put(4 + chunk, y, tn(low[...], slope[:, lanes(y * (ff // 2) + chunk * 384, 384)]))
        return c
    lax.fori_loop(0, 8, up_grad, 0)
    tick("up")
    def first_grad(n, c):
        unit2[:, lanes(n * QUAD, QUAD)] += nt(slope[...], wup[pl.ds(pl.multiple_of(n * QUAD, QUAD), QUAD), :])
        return c
    lax.fori_loop(0, width // QUAD, first_grad, 0)
    def first(n, c):
        r = pl.ds(pl.multiple_of(n * length, length), length)
        d, gain = norm_back(unit1[r, :], inv[0, r, :1], unit2[r, :], ga[...])
        gains[0:1, :] += gain
        unit1[r, :] = d
        dy[r, :] = d.astype(BF16)
        return c
    lax.fori_loop(0, segs, first, 0)
    tick("gains")
    ready("att")
    def proj_grad(y, c):
        put(8, y, tn(att[...], dy[:, lanes(y * 384, 384)]))
        return c
    lax.fori_loop(0, 2, proj_grad, 0)
    tick("proj")
    att[...] = nt(dy[...], wproj[...]).astype(BF16)
    masks = head_mask(length)
    ready("qkv")
    def attend(n, c):
        seg, quad = n // 3, n % 3
        r = pl.ds(pl.multiple_of(seg * length, length), length)
        qs, ks, vs = (lanes(k * width + quad * QUAD, QUAD) for k in range(3))
        da = stacked(att[r, lanes(quad * QUAD, QUAD)], masks)
        q, k = stacked(qkv[r, qs], masks), qkv[r, ks]
        p = probs[n]
        dp = nt(da, qkv[r, vs])
        ds = (p * (dp - jnp.sum(p * dp, -1, keepdims=True))).astype(BF16)
        qkv[r, qs] = (picked(nn(ds, k), masks) * HD ** -0.5).astype(BF16)
        qkv[r, ks] = (tn(ds, q) * HD ** -0.5).astype(BF16)
        qkv[r, vs] = tn(p.astype(BF16), da).astype(BF16)
        return c
    lax.fori_loop(0, 3 * segs, attend, 0)
    tick("attention")
    def in_grad(n, c):
        chunk, y = n // 2, n % 2
        put(9 + chunk, y, tn(x[...], qkv[:, lanes(y * (3 * width // 2) + chunk * 384, 384)]))
        return c
    lax.fori_loop(0, 6, in_grad, 0)
    tick("in")
    def token(n, c):
        s = lanes(n * QUAD, QUAD)
        cot[:, s] = (unit1[:, s] + nt(qkv[...], win[pl.ds(pl.multiple_of(n * QUAD, QUAD), QUAD), :])).astype(BF16)
        return c
    lax.fori_loop(0, width // QUAD, token, 0)
    tick("token")

SAVED = ("qkv", "probs", "att", "unit1", "unit2", "inv", "hidden", "slope")

def backward_kernel(segs, x, cot_h, crossed, w_in, w_proj, w_up, w_down, ga, gf, *rest):
    saved_h, rest = rest[:8], rest[8:]
    token_o, gains_o, g_o = rest[:3]
    cot, win, wproj, wup, wdown = rest[3:8]
    saved = rest[8:16]
    low, dy, g, in_sem, out_sem = rest[16:]
    by = dict(zip(SAVED, zip(saved_h, saved)))
    pairs = [(cot_h, cot), by["unit2"], by["inv"], by["unit1"], by["hidden"], (w_down, wdown), by["slope"], (w_up, wup), by["att"],
             (w_proj, wproj), by["qkv"], by["probs"], (w_in, win)]
    copies = [pltpu.make_async_copy(a, b, in_sem.at[k]) for k, (a, b) in enumerate(pairs)]
    for copy in copies: copy.start()
    groups = {"norms": copies[:4], "hidden": copies[4:5], "slope": copies[5:8], "att": copies[8:10], "qkv": copies[10:]}
    def ready(k):
        for copy in groups[k]: copy.wait()
    out = []
    def tick(k):
        if k == "in":
            copy = pltpu.make_async_copy(g, g_o, out_sem.at[0]); copy.start(); out.append(copy)
        if k == "token":
            copy = pltpu.make_async_copy(cot, token_o, out_sem.at[1]); copy.start(); out.append(copy)
    backward_body(segs, x, cot, crossed, win, wproj, wup, wdown, ga, gf, *saved, low, dy, gains_o, g, ready, tick)
    for copy in out: copy.wait()

def backward(x, cot, crossed, saved, segs, weights):
    w_in, w_proj, ga, w_up, w_down, gf = weights
    rows, width = x.shape
    gs = (NC, 2, 2, 2, 2, 2, 48, 384)
    return pl.pallas_call(
        partial(backward_kernel, segs),
        out_shape=[sds((rows, width), BF16), sds((2, width), F32), sds(gs, BF16)],
        in_specs=[VM, ANY, VM, ANY, ANY, ANY, ANY, VM, VM] + [ANY] * 8,
        out_specs=[ANY, VM, ANY],
        scratch_shapes=[pltpu.VMEM((rows, width), BF16)] + [pltpu.VMEM(w.shape, BF16) for w in (w_in, w_proj, w_up, w_down)]
        + [pltpu.VMEM(s.shape, s.dtype) for s in saved]
        + [pltpu.VMEM((rows, width), BF16), pltpu.VMEM((rows, width), BF16), pltpu.VMEM(gs, BF16),
           pltpu.SemaphoreType.DMA((13,)), pltpu.SemaphoreType.DMA((2,))],
        compiler_params=pltpu.CompilerParams(vmem_limit_bytes=63 << 20),
        name="segment_backward",
    )(x, cot, crossed, w_in, w_proj, w_up, w_down, ga.reshape(1, -1), gf.reshape(1, -1), *saved)

def exact(a, b, dims=(((1,), (0,)), ((), ()))):
    return lax.dot_general(a, b, dims, precision=lax.Precision.HIGHEST, preferred_element_type=F32)

def gather_kernel(mine, out, buf, local, ss, rs):
    y, x, z, core = spots()
    dp, seg = lax.axis_index("dp"), lax.axis_index("seg")
    xn, yn, cn = (2 * y + 1 - x, seg), (2 * (1 - y) + x, seg), (dp, 2 * z + 1 - core)
    zn = [(dp, 2 * lax.rem(z + k, 4) + core) for k in (1, 2, 3)]
    barrier = pltpu.get_barrier_semaphore()
    for d in [xn, yn, cn] + zn:
        pl.semaphore_signal(barrier, inc=1, device_id=d, device_id_type=MESH)
    keep = pltpu.make_async_copy(mine, buf.at[core, x, y, z], local.at[0])
    keep.start()
    pl.semaphore_wait(barrier, 6)
    def send(src, dst, k, to):
        return pltpu.make_async_remote_copy(src, dst, ss.at[k], rs.at[k], device_id=to, device_id_type=MESH)
    stage = [send(mine, buf.at[core, x, y, z], k, zn[k]) for k in range(3)]
    for s in stage: s.start()
    keep.wait()
    for s in stage: s.wait()
    for k, part, to in ((3, buf.at[core, x, y], yn), (4, buf.at[core, x], xn), (5, buf.at[core], cn)):
        s = send(part, part, k, to)
        s.start(); s.wait()
    copy = pltpu.make_async_copy(buf, out, local.at[1])
    copy.start(); copy.wait()

def gather(mine, cid):
    shape = (2, 2, 2, 4) + mine.shape
    return pl.pallas_call(
        gather_kernel, out_shape=sds(shape, mine.dtype), in_specs=[VM], out_specs=ANY,
        scratch_shapes=[pltpu.VMEM(shape, mine.dtype), pltpu.SemaphoreType.DMA((2,)), pltpu.SemaphoreType.DMA((6,)), pltpu.SemaphoreType.DMA((6,))],
        compiler_params=pltpu.CompilerParams(collective_id=cid, has_side_effects=True), name="gather_first_rows")(mine)

def row_spots(shape, axis):
    r = lax.broadcasted_iota(jnp.int32, shape, axis)
    core, x, y, z, s = r // 64, r // 32 % 2, r // 16 % 2, r // 4 % 4, r % 4
    return 2 * y + x, s * 8 + 2 * z + core

def row_docs(shape, axis, counts):
    slot, place = row_spots(shape, axis)
    document, begin, first = jnp.zeros(shape, jnp.int32), jnp.zeros(shape, jnp.int32), jnp.zeros(shape, jnp.int32)
    for s in range(counts.shape[0]):
        end = jnp.int32(0)
        for d in range(counts.shape[1]):
            start, end = end, end + counts[s, d]
            here = slot == s
            document += jnp.where(here & (end <= place), 1, 0)
            begin = jnp.where(here & (start <= place) & (place < end), start, begin)
            first = jnp.where(here & (start == place), 1, first)
    return slot, place, document, place - begin, first

def cross_kernel(rows_in, counts, pads, embed, w_in, w_proj, w_up, w_down, ga, gf,
                 result_o, crossed_o, d_in, d_proj, d_up, d_down, gains_o, embed_o,
                 win, wproj, wup, wdown, hidden, slope, grad_pre, acc, base, cot, sem):
    loads = [pltpu.make_async_copy(a, b, sem.at[k]) for k, (a, b) in enumerate(((w_in, win), (w_proj, wproj), (w_up, wup), (w_down, wdown)))]
    for load in loads: load.start()
    cross_body(rows_in, counts, pads, embed, win, wproj, wup, wdown, ga, gf, result_o, crossed_o, d_in, d_proj, d_up, d_down, gains_o, embed_o,
               hidden, slope, grad_pre, acc, base, cot, lambda k: loads[k].wait())

def cross_body(rows_in, counts, pads, embed, win, wproj, wup, wdown, ga, gf, result_o, crossed_o, d_in, d_proj, d_up, d_down, gains_o, embed_o,
               hidden, slope, grad_pre, acc, base, cot, ready):
    y, x, z, core = spots()
    width = embed.shape[1]
    n = 128
    for k in range(32):
        at = rows_in.at[k // 16, k // 8 % 2, k // 4 % 2, k % 4]
        base[4 * k : 4 * k + 4, :] = at[:, :width]
        cot[4 * k : 4 * k + 4, :] = at[:, width:]
    slot_c, place_c, doc_c, rank_c, first_c = row_docs((n, 1), 0, counts)
    slot_r, place_r, doc_r, rank_r, first_r = row_docs((1, n), 1, counts)
    places = lax.broadcasted_iota(jnp.int32, (32, n), 0)
    by_slot = exact(pads[...].astype(F32), (places == place_r).astype(F32))
    pad_r = jnp.zeros((1, n), F32)
    for s in range(pads.shape[0]):
        pad_r = jnp.where(slot_r == s, by_slot[s : s + 1], pad_r)
    ok_r = (pad_r == 0) | (first_r == 1)
    allowed = (slot_c == slot_r) & (doc_c == doc_r) & ok_r
    pick = (rank_c == lax.broadcasted_iota(jnp.int32, (n, 32), 1)).astype(F32)
    xin = base[...] + exact(pick, embed[...])
    xl = xin.astype(BF16)
    masks = head_mask(n)
    wide = jnp.concatenate([allowed.astype(F32)] * 4, 0) > 0
    ready(0)
    qkv = jnp.concatenate([nn(xl, win[:, k * width : (k + 1) * width]).astype(BF16) for k in range(3)], 1)
    probs, atts = [], []
    part = lambda a, k, quad: a[:, k * width + quad * QUAD : k * width + quad * QUAD + QUAD]
    for quad in range(3):
        scores = jnp.where(wide, nt(stacked(part(qkv, 0, quad), masks), part(qkv, 1, quad)) * HD ** -0.5, MASKED)
        e = jnp.exp(scores - jnp.max(scores, -1, keepdims=True))
        p = e / jnp.sum(e, -1, keepdims=True)
        probs.append(p)
        atts.append(picked(nn(p.astype(BF16), part(qkv, 2, quad)), masks).astype(BF16))
    att = jnp.concatenate(atts, 1)
    ready(1)
    u1, i1 = unit(xin + nn(att, wproj[...]))
    f = u1 * ga[...]
    fl = f.astype(BF16)
    ready(2)
    ff, tile = wup.shape[1], 512
    def up(k, c):
        s = lanes(k * tile, tile)
        h, g = gelu_pair(nn(fl, wup[:, s]))
        hidden[:, s] = h.astype(BF16)
        slope[:, s] = g
        return c
    lax.fori_loop(0, ff // tile, up, 0)
    ready(3)
    u2, i2 = unit(f + nn(hidden[...], wdown[...]))
    me = ((core * 2 + x) * 2 + y) * 4 + z
    own = (lax.broadcasted_iota(jnp.int32, (8, n), 1) == 4 * me + lax.broadcasted_iota(jnp.int32, (8, n), 0)).astype(F32)
    result_o[...] = exact(own, u2 * gf[...])
    d2, gain_f = norm_back(u2, i2, cot[...], gf[...])
    dy2 = d2.astype(BF16)
    def pre(k, c):
        s = lanes(k * tile, tile)
        grad_pre[:, s] = (nt(dy2, wdown[pl.ds(pl.multiple_of(k * tile, tile), tile), :]) * slope[:, s]).astype(BF16)
        return c
    lax.fori_loop(0, ff // tile, pre, 0)
    d1, gain_a = norm_back(u1, i1, d2 + nt(grad_pre[...], wup[...]), ga[...])
    dy1 = d1.astype(BF16)
    datt = nt(dy1, wproj[...]).astype(BF16)
    dq, dk, dv = [], [], []
    for quad in range(3):
        da = stacked(part(datt, 0, quad), masks)
        q, k = stacked(part(qkv, 0, quad), masks), part(qkv, 1, quad)
        p = probs[quad]
        dp = nt(da, part(qkv, 2, quad))
        ds = (p * (dp - jnp.sum(p * dp, -1, keepdims=True))).astype(BF16)
        dq.append((picked(nn(ds, k), masks) * HD ** -0.5).astype(BF16))
        dk.append((tn(ds, q) * HD ** -0.5).astype(BF16))
        dv.append(tn(p.astype(BF16), da).astype(BF16))
    dqkv = jnp.concatenate(dq + dk + dv, 1)
    crossed = d1 + nt(dqkv, win[...])
    crossed_o[...] = exact(own, crossed)
    gains_o[0:1, :] = gain_a
    gains_o[1:2, :] = gain_f
    embed_o[...] = exact(pick, crossed, (((0,), (0,)), ((), ())))
    j, i = 2 * z + core, 2 * y + x
    def turn(a, by):
        a = a.astype(F32)
        return pltpu.roll(a, lax.rem(a.shape[1] - by, a.shape[1]), 1).astype(BF16)
    sixth = width // 8
    left = lambda a: turn(a, sixth * j)[:, :128]
    d_in[...] = tn(left(xl), turn(dqkv, 3 * width // 4 * i)[:, :640])[:sixth, : 3 * width // 4]
    d_proj[...] = tn(left(att), turn(dy1, width // 4 * i)[:, :256])[:sixth, : width // 4]
    d_up[...] = tn(left(fl), grad_pre[:, lanes(ff // 4 * i, ff // 4)])[:sixth]
    d_down[...] = tn(hidden[:, lanes(ff // 8 * j, ff // 8)], turn(dy2, width // 4 * i)[:, :256])[:, : width // 4]

def cross(rows, counts, pads, embed, weights):
    w_in, w_proj, ga, w_up, w_down, gf = weights
    width, ff, n = embed.shape[1], w_up.shape[1], 128
    outs = [((8, width), F32)] * 2 + [((width // 8, 3 * width // 4), F32), ((width // 8, width // 4), F32), ((width // 8, ff // 4), F32),
            ((ff // 8, width // 4), F32), ((2, width), F32), (embed.shape, F32)]
    return pl.pallas_call(
        cross_kernel, out_shape=[sds(*o) for o in outs],
        in_specs=[VM, pl.BlockSpec(memory_space=pltpu.SMEM), VM, VM, ANY, ANY, ANY, ANY, VM, VM], out_specs=[VM] * len(outs),
        scratch_shapes=[pltpu.VMEM(w.shape, BF16) for w in (w_in, w_proj, w_up, w_down)]
        + [pltpu.VMEM((n, ff), BF16), pltpu.VMEM((n, ff), F32), pltpu.VMEM((n, ff), BF16)] + [pltpu.VMEM((n, width), F32)] * 3 + [pltpu.SemaphoreType.DMA((4,))],
        compiler_params=pltpu.CompilerParams(vmem_limit_bytes=60 << 20), name="cross_block",
    )(rows, counts, pads, embed, w_in, w_proj, w_up, w_down, ga.reshape(1, -1), gf.reshape(1, -1))


class Reducer:
    def __init__(self, g, bufs):
        self.g = g
        self.r1, self.r2, self.r3, self.r4, self.own, self.peer, self.gain, self.ss, self.rs, self.zs, self.zr, self.gs, self.gr = bufs
        self.y, self.x, self.z, self.core = y, x, z, core = spots()
        self.dp, self.seg = lax.axis_index("dp"), lax.axis_index("seg")
        self.xn, self.yn, self.cn = (2 * y + 1 - x, self.seg), (2 * (1 - y) + x, self.seg), (self.dp, 2 * z + 1 - core)
        self.zt = [lax.rem(z + k, 4) for k in (1, 2, 3)]
        self.zn = [(self.dp, 2 * t + core) for t in self.zt]
        self.order = ((x, y, self.xn, self.yn), (y, x, self.yn, self.xn))

    @staticmethod
    def scratch(width):
        dma = pltpu.SemaphoreType.DMA
        v = lambda *s: pltpu.VMEM(s + (48, 384), BF16)
        return [v(NC, 2, 2, 2, 2), v(NC, 2, 2, 2), v(NC, 4), v(NC, 3), v(NC), v(NC), pltpu.VMEM((7, 2, width), F32),
                dma((6, NC)), dma((6, NC)), dma((3, NC)), dma((3, NC)), dma((6,)), dma((6,))]

    def greet(self):
        barrier = pltpu.get_barrier_semaphore()
        for d in [self.xn, self.yn, self.cn] + self.zn:
            pl.semaphore_signal(barrier, inc=1, device_id=d, device_id_type=MESH)
    def met(self):
        pl.semaphore_wait(pltpu.get_barrier_semaphore(), 6)

    def copy(self, src, dst, s, r, to):
        return pltpu.make_async_remote_copy(src, dst, s, r, device_id=to, device_id_type=MESH)
    def s1(self, c):
        return self.copy(self.g.at[c, 1 - self.core], self.r1.at[c], self.ss.at[0, c], self.rs.at[0, c], self.cn)
    def s2(self, c, h):
        p, q, pn, qn = self.order[h]
        return self.copy(self.r1.at[c, h, 1 - p], self.r2.at[c, h], self.ss.at[1 + h, c], self.rs.at[1 + h, c], pn)
    def s3(self, c, h):
        p, q, pn, qn = self.order[h]
        return self.copy(self.r2.at[c, h, 1 - q], self.r3.at[c, pl.ds(2 * h, 2)], self.ss.at[3 + h, c], self.rs.at[3 + h, c], qn)
    def s4(self, c, k):
        return self.copy(self.r3.at[c, self.zt[k]], self.r4.at[c, k], self.zs.at[k, c], self.zr.at[k, c], self.zn[k])
    def s5(self, c):
        return self.copy(self.own.at[c], self.peer.at[c], self.ss.at[5, c], self.rs.at[5, c], self.xn)
    def needs(self, c, x):
        low = (c == 4) | (c == 5) | (c == 9)
        high = (c == 6) | (c == 7) | (c == 11)
        return jnp.logical_not((low & (x == 1)) | (high & (x == 0)))

    @staticmethod
    def add(*terms):
        total = terms[0].astype(F32)
        for t in terms[1:]:
            total = total + t.astype(F32)
        return total.astype(BF16)

    def start(self, c):
        self.s1(c).start()
    def core_done(self, c):
        self.s1(c).wait()
        for h in (0, 1):
            p = self.order[h][0]
            self.r1[c, h, 1 - p] = self.add(self.g[c, self.core, h, 1 - p], self.r1[c, h, 1 - p])
            self.s2(c, h).start()
        for h in (0, 1):
            p = self.order[h][0]
            self.r1[c, h, p] = self.add(self.g[c, self.core, h, p], self.r1[c, h, p])
    def first_done(self, c):
        for h in (0, 1):
            self.s2(c, h).wait()
            self.r2[c, h] = self.add(self.r1[c, h, self.order[h][0]], self.r2[c, h])
            self.s3(c, h).start()
    def second_done(self, c):
        for h in (0, 1):
            self.s3(c, h).wait()
            rows = pl.ds(2 * h, 2)
            self.r3[c, rows] = self.add(self.r2[c, h, self.order[h][1]], self.r3[c, rows])
        for k in range(3): self.s4(c, k).start()
    def line_done(self, c):
        for k in range(3): self.s4(c, k).wait()
        self.own[c] = self.add(self.r3[c, self.z], self.r4[c, 0], self.r4[c, 1], self.r4[c, 2])
        @pl.when(self.needs(c, 1 - self.x))
        def _(): self.s5(c).start()
    def swap_done(self, c):
        @pl.when(self.needs(c, 1 - self.x))
        def _(): self.s5(c).wait_send()
        @pl.when(self.needs(c, self.x))
        def _(): self.s5(c).wait_recv()

    def advance(self, t):
        for stage, act in enumerate((self.start, self.core_done, self.first_done, self.second_done, self.line_done, self.swap_done)):
            @pl.when((t >= stage) & (t < NC + stage))
            def _(): act(t - stage)

    def gain_copies(self, stage):
        if stage < 3:
            to = (self.cn, self.xn, self.yn)[stage]
            return [self.copy(self.gain.at[0], self.gain.at[1 + stage], self.gs.at[stage], self.gr.at[stage], to)]
        return [self.copy(self.gain.at[0], self.gain.at[4 + k], self.gs.at[3 + k], self.gr.at[3 + k], self.zn[k]) for k in range(3)]
    def gain_start(self, stage):
        for c in self.gain_copies(stage): c.start()
    def gain_done(self, stage):
        for c in self.gain_copies(stage): c.wait()
        if stage < 3:
            self.gain[0] = self.gain[0] + self.gain[1 + stage]
        else:
            self.gain[0] = self.gain[0] + self.gain[4] + self.gain[5] + self.gain[6]

    def deliver(self, d_in, d_proj, d_up, d_down):
        for mine in (0, 1):
            @pl.when(self.x == mine)
            def _():
                for half in (0, 1):
                    a = self.own if half == mine else self.peer
                    r = slice(48 * half, 48 * half + 48)
                    side = slice(192 * mine, 192 * mine + 192)
                    d_proj[r, :] = a[8, :, side].astype(F32)
                    for k in range(2):
                        d_up[r, 384 * k : 384 * k + 384] = a[4 + 2 * mine + k].astype(F32)
                    parts = [a[9], a[10, :, side]] if mine == 0 else [a[10, :, side], a[11]]
                    d_in[r, :] = jnp.concatenate(parts, 1).astype(F32)
                    for k in range(4):
                        d_down[96 * k + 48 * half : 96 * k + 48 * half + 48, :] = a[k, :, side].astype(F32)

def reduce_kernel(g_in, gains, d_in, d_proj, d_up, d_down, gains_o, *scr):
    red = Reducer(g_in, scr)
    red.greet()
    red.gain[0] = gains[...]
    red.met()
    def step(t, c):
        red.advance(t)
        return c
    lax.fori_loop(0, 3, step, 0)
    for k in range(4):
        red.gain_start(k)
        lax.fori_loop(3 + 3 * k, 6 + 3 * k, step, 0)
        red.gain_done(k)
    lax.fori_loop(15, NC + 6, step, 0)
    gains_o[...] = red.gain[0]
    red.deliver(d_in, d_proj, d_up, d_down)

def reduce(g, gains, width, ff):
    outs = [(width // 8, 3 * width // 4), (width // 8, width // 4), (width // 8, ff // 4), (ff // 8, width // 4), (2, width)]
    return pl.pallas_call(
        reduce_kernel, out_shape=[sds(s, F32) for s in outs], in_specs=[VM, VM], out_specs=[VM] * 5, scratch_shapes=Reducer.scratch(width),
        compiler_params=pltpu.CompilerParams(collective_id=1, has_side_effects=True, vmem_limit_bytes=60 << 20), name="reduce_weights")(g, gains)


def this_mesh(
    tokens, doc_counts, pad_mask, attn_in, attn_proj, norm_attn, ffn_up, ffn_down, norm_ffn,
    segment_embed, cross_in, cross_proj, cross_norm_attn, cross_up, cross_down, cross_norm_ffn,
    cotangent,
):
    segs, length, width = tokens.shape
    rows, ff = segs * length, ffn_up.shape[1]
    member, group = lax.axis_index("seg"), lax.axis_index("dp")
    x, cot = tokens.reshape(rows, width), cotangent.reshape(rows, width)
    weights = (attn_in, attn_proj, norm_attn, ffn_up, ffn_down, norm_ffn)
    cross_weights = (cross_in, cross_proj, cross_norm_attn, cross_up, cross_down, cross_norm_ffn)
    *saved, out, first = forward(x, segs, weights)
    mine = jnp.concatenate([first, cotangent[:, 0, :].astype(F32)], 1)
    everyone = gather(mine, 0)
    result, crossed, c_in, c_proj, c_up, c_down, c_gains, c_embed = cross(everyone, doc_counts, pad_mask, segment_embed, cross_weights)
    output = out.reshape(tokens.shape).at[:, 0, :].set(result[:segs].astype(BF16))
    token_grad, gains, g = backward(x, cot, crossed, saved, segs, weights)
    d_in, d_proj, d_up, d_down, totals = reduce(g, gains, width, ff)
    block = width // 8
    piece = lambda a, k: lax.dynamic_slice(a, (k, member * block), (1, block))[0]
    embed_block = lax.dynamic_slice(c_embed, (group * 8, member * block), (8, block))
    return (
        output, token_grad.reshape(tokens.shape), d_in, d_proj, piece(totals, 0), d_up, d_down, piece(totals, 1),
        embed_block, c_in, c_proj, piece(c_gains, 0), c_up, c_down, piece(c_gains, 1),
    )


def solution(mesh):
    fits = (mesh.shape["dp"], mesh.shape["seg"]) == (4, 8)
    placed = (
        P(("dp", "seg"), None, None),
        P(),
        P(),
        P(),
        P(),
        P(),
        P(),
        P(),
        P(),
        P(),
        P(),
        P(),
        P(),
        P(),
        P(),
        P(),
        P(("dp", "seg"), None, None),
    )
    return jax.shard_map(
        this_mesh if fits else any_mesh,
        mesh=mesh,
        in_specs=placed,
        out_specs=(
            P(("dp", "seg"), None, None),
            P(("dp", "seg"), None, None),
            P("seg", "dp"),
            P("seg", "dp"),
            P("seg"),
            P("seg", "dp"),
            P("seg", "dp"),
            P("seg"),
            P("dp", "seg"),
            P("seg", "dp"),
            P("seg", "dp"),
            P("seg"),
            P("seg", "dp"),
            P("seg", "dp"),
            P("seg"),
        ),
        check_vma=False,
    )
```

```python
from functools import partial

import jax
import jax.numpy as jnp
import numpy as np
from jax.experimental import pallas as pl
from jax.experimental.pallas import tpu as pltpu
from jax import lax
from jax.sharding import PartitionSpec as P

H = 12
HD = 64
SLOT_SEGS = 32


EPSILON = 1e-05
MASKED = -1e30


def matmul(former, latter):
    return jnp.dot(former, latter, preferred_element_type=jnp.float32)


def exact_dot(former, latter):
    return jnp.dot(former, latter, precision=lax.Precision.HIGHEST)


def outer_sum(former, latter):
    return lax.dot_general(
        former, latter, (((0,), (0,)), ((), ())), preferred_element_type=jnp.float32
    )


def back_product(gradient, weight):
    return lax.dot_general(
        gradient, weight, (((1,), (1,)), ((), ())), preferred_element_type=jnp.float32
    )


def norm_forward(summed, gain_row):
    middle = summed - jnp.mean(summed, -1, keepdims=True)
    inverse = lax.rsqrt(jnp.mean(middle * middle, -1, keepdims=True) + EPSILON)
    unit_rows = middle * inverse
    return (unit_rows * gain_row, (unit_rows, inverse))


def norm_backward(state, gain_row, upstream):
    unit_rows, inverse = state
    scaled = upstream * gain_row
    centered = (
        scaled
        - jnp.mean(scaled, -1, keepdims=True)
        - unit_rows * jnp.mean(scaled * unit_rows, -1, keepdims=True)
    )
    return (inverse * centered, jnp.sum(upstream * unit_rows, 0))


def to_heads(columns, batch_size):
    return columns.reshape(batch_size, -1, H, HD)


def attend_forward(queries, key_heads, values, allowed):
    scores = jnp.einsum(
        "bqhe,bkhe->bhqk", queries, key_heads, preferred_element_type=jnp.float32
    ) * HD ** (-0.5)
    if allowed is not None:
        scores = jnp.where(allowed, scores, MASKED)
    attn_probs = jax.nn.softmax(scores, axis=-1)
    probs_low = attn_probs.astype(jnp.bfloat16)
    attended = jnp.einsum("bhqk,bkhe->bqhe", probs_low, values, preferred_element_type=jnp.float32)
    return (attn_probs, probs_low, attended.astype(jnp.bfloat16))


def score_grads(attn_probs, grad_att, values):
    grad_probs = jnp.einsum("bqhe,bkhe->bhqk", grad_att, values, preferred_element_type=jnp.float32)
    return (attn_probs * (grad_probs - jnp.sum(attn_probs * grad_probs, -1, keepdims=True))).astype(
        jnp.bfloat16
    )


def tail_forward(residual, attended, weights):
    attn_proj, norm_attn, ffn_up, ffn_down, norm_ffn = weights
    first_norm, first_state = norm_forward(residual + matmul(attended, attn_proj), norm_attn)
    first_low = first_norm.astype(jnp.bfloat16)
    pre_act = matmul(first_low, ffn_up)
    hidden = jax.nn.gelu(pre_act, approximate=False).astype(jnp.bfloat16)
    result, second_state = norm_forward(first_norm + matmul(hidden, ffn_down), norm_ffn)
    return (result, (attended, first_state, first_low, pre_act, hidden, second_state))


def tail_backward(state, weights, upstream):
    attn_proj, norm_attn, ffn_up, ffn_down, norm_ffn = weights
    attended, first_state, first_low, pre_act, hidden, second_state = state
    grad_second, grad_norm_ffn = norm_backward(second_state, norm_ffn, upstream)
    grad_out_low = grad_second.astype(jnp.bfloat16)
    grad_down = outer_sum(hidden, grad_out_low)
    spare, gelu_back = jax.vjp(partial(jax.nn.gelu, approximate=False), pre_act)
    grad_pre = gelu_back(back_product(grad_out_low, ffn_down))[0].astype(jnp.bfloat16)
    grad_up = outer_sum(first_low, grad_pre)
    grad_first = grad_second + back_product(grad_pre, ffn_up)
    grad_residual, grad_norm_attn = norm_backward(first_state, norm_attn, grad_first)
    grad_proj_out = grad_residual.astype(jnp.bfloat16)
    grad_proj = outer_sum(attended, grad_proj_out)
    grad_att = back_product(grad_proj_out, attn_proj).astype(jnp.bfloat16)
    grads = (grad_proj, grad_norm_attn, grad_up, grad_down, grad_norm_ffn)
    factors = (attended, grad_proj_out, first_low, grad_pre, hidden, grad_out_low)
    return (grad_residual, grad_att, grads, factors)


def segment_forward(token_rows, seg_count, weights):
    attn_in = weights[0]
    model_width = token_rows.shape[1]
    packed = matmul(token_rows, attn_in).astype(jnp.bfloat16)
    queries = to_heads(packed[:, :model_width], seg_count)
    key_heads = to_heads(packed[:, model_width : 2 * model_width], seg_count)
    values = to_heads(packed[:, 2 * model_width :], seg_count)
    attn_probs, probs_low, attended = attend_forward(queries, key_heads, values, None)
    result, state = tail_forward(
        token_rows.astype(jnp.float32), attended.reshape(token_rows.shape), weights[1:]
    )
    return (result, (queries, key_heads, values, attn_probs, probs_low, state))


def row_places(groups, members, seg_count):
    span_devs = SLOT_SEGS // seg_count
    group_slots = members // span_devs
    half_count = seg_count // 2
    row = np.arange(groups * members * seg_count)
    device, within = row // seg_count, row % seg_count
    group, member = device // members, device % members
    slot = group * group_slots + (
        member // span_devs + within % half_count + group_slots // 2 * (within // half_count)
    ) % group_slots
    return slot, within * span_devs + member % span_devs


def documents(doc_counts, pad_mask):
    doc_ends = jnp.cumsum(doc_counts, 1)
    doc_starts = doc_ends - doc_counts
    places = jnp.arange(pad_mask.shape[1], dtype=jnp.int32)
    document = jnp.sum((doc_ends[:, None, :] <= places[None, :, None]).astype(jnp.int32), 2)
    is_first = jnp.any(doc_starts[:, None, :] == places[None, :, None], 2)
    doc_index = jnp.arange(doc_counts.shape[1], dtype=jnp.int32)
    doc_begin = jnp.sum(
        jnp.where(doc_index[None, None] == document[:, :, None], doc_starts[:, None, :], 0), 2
    )
    return document, places[None] - doc_begin, (pad_mask == 0) | is_first


def cross_section(base, cot_rows, embed_pick, allowed, segment_embed, weights):
    cross_in = weights[0]
    tail_weights = weights[1:]
    rows, width = base.shape
    slots = rows // SLOT_SEGS
    cross_input = base + exact_dot(embed_pick, segment_embed)
    cross_low = cross_input.astype(jnp.bfloat16)
    packed = matmul(cross_low, cross_in).astype(jnp.bfloat16)
    queries = to_heads(packed[:, :width], slots)
    keys = to_heads(packed[:, width : 2 * width], slots)
    values = to_heads(packed[:, 2 * width :], slots)
    probs, probs_low, attended = attend_forward(queries, keys, values, allowed)
    result, state = tail_forward(cross_input, attended.reshape(rows, width), tail_weights)
    grad_in, grad_att, tail_grads, factors = tail_backward_factors(state, tail_weights, cot_rows)
    grad_packed = attend_backward(probs, probs_low, queries, keys, values, to_heads(grad_att, slots), rows)
    grad_input = grad_in + back_product(grad_packed, cross_in)
    return result, grad_input, (cross_low, grad_packed) + factors, tail_grads


def attend_backward(probs, probs_low, queries, keys, values, grad_att, rows):
    scores_grad = score_grads(probs, grad_att, values)
    grad_query = jnp.einsum("bhqk,bkhe->bqhe", scores_grad, keys, preferred_element_type=jnp.float32) * HD ** (-0.5)
    grad_key = jnp.einsum("bhqk,bqhe->bkhe", scores_grad, queries, preferred_element_type=jnp.float32) * HD ** (-0.5)
    grad_value = jnp.einsum("bhqk,bqhe->bkhe", probs_low, grad_att, preferred_element_type=jnp.float32)
    return jnp.concatenate([g.reshape(rows, H * HD) for g in (grad_query, grad_key, grad_value)], 1).astype(jnp.bfloat16)


def tail_backward_factors(state, weights, upstream):
    attn_proj, norm_attn, ffn_up, ffn_down, norm_ffn = weights
    attended, first_state, first_low, pre_act, hidden, second_state = state
    grad_second, grad_norm_ffn = norm_backward(second_state, norm_ffn, upstream)
    grad_out_low = grad_second.astype(jnp.bfloat16)
    spare, gelu_back = jax.vjp(partial(jax.nn.gelu, approximate=False), pre_act)
    grad_pre = gelu_back(back_product(grad_out_low, ffn_down))[0].astype(jnp.bfloat16)
    grad_first = grad_second + back_product(grad_pre, ffn_up)
    grad_residual, grad_norm_attn = norm_backward(first_state, norm_attn, grad_first)
    grad_proj_out = grad_residual.astype(jnp.bfloat16)
    grad_att = back_product(grad_proj_out, attn_proj).astype(jnp.bfloat16)
    factors = (attended, grad_proj_out, first_low, grad_pre, hidden, grad_out_low)
    return grad_residual, grad_att, (grad_norm_attn, grad_norm_ffn), factors


def reduce_weights(grads, groups, members):
    parts = [lax.psum_scatter(g.astype(jnp.bfloat16), "seg", scatter_dimension=0, tiled=True) for g in grads]
    flat = [p.reshape(p.shape[0], groups, -1).transpose(1, 0, 2).reshape(groups, -1) for p in parts]
    joined = lax.psum_scatter(jnp.concatenate(flat, 1), "dp", scatter_dimension=0, tiled=True)[0].astype(jnp.float32)
    outs, at = [], 0
    for p in parts:
        rows, columns = p.shape[0], p.shape[1] // groups
        outs.append(joined[at : at + rows * columns].reshape(rows, columns))
        at += rows * columns
    return outs


def any_mesh(
    tokens, doc_counts, pad_mask, attn_in, attn_proj, norm_attn, ffn_up, ffn_down, norm_ffn,
    segment_embed, cross_in, cross_proj, cross_norm_attn, cross_up, cross_down, cross_norm_ffn,
    cotangent,
):
    seg_count, seg_length, width = tokens.shape
    rows = seg_count * seg_length
    members, groups = lax.axis_size("seg"), lax.axis_size("dp")
    member, group = lax.axis_index("seg"), lax.axis_index("dp")
    device = group * members + member
    token_rows = tokens.reshape(rows, width)
    seg_weights = (attn_in, attn_proj, norm_attn, ffn_up, ffn_down, norm_ffn)
    cross_weights = (cross_in, cross_proj, cross_norm_attn, cross_up, cross_down, cross_norm_ffn)

    slot_of, place_of = row_places(groups, members, seg_count)
    order = np.argsort(slot_of * SLOT_SEGS + place_of)
    slots = pad_mask.shape[0]
    document, rank, key_ok = documents(doc_counts, pad_mask)
    allowed = (document[:, :, None] == document[:, None, :]) & key_ok[:, None, :]
    embed_pick = (
        rank.reshape(-1)[:, None] == jnp.arange(segment_embed.shape[0], dtype=jnp.int32)[None]
    ).astype(jnp.float32)

    cot_first = lax.all_gather(cotangent[:, 0, :], ("dp", "seg"), axis=0, tiled=True)[order]
    seg_result, seg_state = segment_forward(token_rows, seg_count, seg_weights)
    seg_cube = seg_result.reshape(seg_count, seg_length, width)
    base = lax.all_gather(seg_cube[:, 0, :], ("dp", "seg"), axis=0, tiled=True)[order]
    cross_result, cross_grad, factors, cross_gains = cross_section(
        base, cot_first.astype(jnp.float32), embed_pick, allowed[:, None], segment_embed, cross_weights
    )
    back = np.argsort(order)
    own = lambda a: lax.dynamic_slice_in_dim(a[back], device * seg_count, seg_count, 0)
    output = jnp.concatenate(
        [own(cross_result.astype(jnp.bfloat16))[:, None, :], seg_cube[:, 1:, :].astype(jnp.bfloat16)], 1
    )

    def share(left, right):
        r, c = left.shape[1] // members, right.shape[1] // groups
        return outer_sum(
            lax.dynamic_slice_in_dim(left, member * r, r, 1), lax.dynamic_slice_in_dim(right, group * c, c, 1)
        )

    cross_low, cross_packed, cross_att, cross_proj_out, cross_first, cross_pre, cross_hidden, cross_out = factors
    grad_cross_in = share(cross_low, cross_packed)
    grad_cross_proj = share(cross_att, cross_proj_out)
    grad_cross_up = share(cross_first, cross_pre)
    grad_cross_down = share(cross_hidden, cross_out)
    er, ec = segment_embed.shape[0] // groups, width // members
    grad_embed = lax.dot_general(
        lax.dynamic_slice_in_dim(embed_pick, group * er, er, 1),
        lax.dynamic_slice_in_dim(cross_grad, member * ec, ec, 1),
        (((0,), (0,)), ((), ())), precision=lax.Precision.HIGHEST,
    )
    piece = lambda g: lax.dynamic_slice_in_dim(g, member * ec, ec, 0)

    upstream = cotangent.astype(jnp.float32)
    seg_upstream = jnp.concatenate([own(cross_grad)[:, None, :], upstream[:, 1:, :]], 1).reshape(rows, width)
    queries, key_heads, values, attn_probs, probs_low, tail_state = seg_state
    grad_residual, grad_att, seg_tail_grads, spare = tail_backward(tail_state, seg_weights[1:], seg_upstream)
    grad_packed = attend_backward(
        attn_probs, probs_low, queries, key_heads, values, to_heads(grad_att, seg_count), rows
    )
    grad_attn_in = outer_sum(token_rows, grad_packed)
    token_grad = (grad_residual + back_product(grad_packed, attn_in)).astype(jnp.bfloat16).reshape(tokens.shape)
    grad_attn_proj, grad_norm_attn, grad_ffn_up, grad_ffn_down, grad_norm_ffn = seg_tail_grads
    total_in, total_proj, total_up, total_down = reduce_weights(
        (grad_attn_in, grad_attn_proj, grad_ffn_up, grad_ffn_down), groups, members
    )
    gains = lax.psum(jnp.concatenate([grad_norm_attn, grad_norm_ffn]), ("dp", "seg"))
    return (
        output, token_grad, total_in, total_proj, piece(gains[:width]), total_up, total_down,
        piece(gains[width:]), grad_embed, grad_cross_in, grad_cross_proj, piece(cross_gains[0]),
        grad_cross_up, grad_cross_down, piece(cross_gains[1]),
    )


BF16, F32 = jnp.bfloat16, jnp.float32
QUAD = 4 * HD
NC, GS = 12, 8
PAY = 3 * 768 + 128
MESH = pl.DeviceIdType.MESH
ERFC = (0.23192104, 0.16183046, 0.46825631, -0.37088501, 0.70913273, -0.20025555)

def nn(a, b): return jnp.dot(a, b, preferred_element_type=F32)
def nt(a, b): return lax.dot_general(a, b, (((1,), (1,)), ((), ())), preferred_element_type=F32)
def tn(a, b): return lax.dot_general(a, b, (((0,), (0,)), ((), ())), preferred_element_type=F32)

def gelu_pair(v):
    size = jnp.abs(v)
    t = 1.0 / (1.0 + (0.4 * 0.5 ** 0.5) * size)
    bell = jnp.exp(-0.5 * (v * v))
    poly = F32(0.5 * ERFC[5])
    for c in ERFC[4::-1]:
        poly = poly * t + F32(0.5 * c)
    tail = poly * t * bell
    cdf = jnp.where(v >= 0, 1.0 - tail, tail)
    scaled = v * cdf
    return scaled, cdf + v * (bell * F32((2 * np.pi) ** -0.5))

def mean(v): return jnp.mean(v, -1, keepdims=True)

def unit(total):
    middle = total - mean(total)
    inverse = lax.rsqrt(mean(middle * middle) + EPSILON)
    return middle * inverse, inverse

def lanes(start, size):
    return pl.ds(pl.multiple_of(start, 128), size)

def head_mask(rows):
    lane = lax.broadcasted_iota(jnp.int32, (rows, QUAD), 1)
    return [lane // HD == h for h in range(4)]

def stacked(v, masks):
    zero = jnp.zeros_like(v)
    return jnp.concatenate([jnp.where(m, v, zero) for m in masks], 0)

def picked(v, masks):
    n = v.shape[0] // 4
    out = v[3 * n :]
    for h in (2, 1, 0):
        out = jnp.where(masks[h], v[h * n : (h + 1) * n], out)
    return out

def row(v):
    return v[...].reshape(1, v.shape[0])

def forward_kernel(segs, x, w_in, w_proj, w_up, w_down, ga_v,
                   qkv_o, probs_o, att_o, unit1_o, unit2_o, inv_o, hidden_o, slope_o,
                   win, wproj, wup, wdown, qkv, probs, att, unit1, unit2, inv, hidden, slope, acc, low, in_sem, out_sem):
    rows, width = x.shape
    length = rows // segs
    ga = row(ga_v)
    loads = [pltpu.make_async_copy(a, b, in_sem.at[k]) for k, (a, b) in enumerate(((w_in, win), (w_proj, wproj), (w_up, wup), (w_down, wdown)))]
    for load in loads: load.start()
    saves = []
    def save(a, b):
        copy = pltpu.make_async_copy(a, b, out_sem.at[len(saves)])
        copy.start(); saves.append(copy)
    loads[0].wait()
    def project(n, c):
        s = lanes(n * width, width)
        qkv[:, s] = nn(x[...], win[:, s]).astype(BF16)
        return c
    lax.fori_loop(0, 3, project, 0)
    save(qkv, qkv_o)
    masks = head_mask(length)
    def attend(n, c):
        seg, quad = n // 3, n % 3
        r = pl.ds(pl.multiple_of(seg * length, length), length)
        q = stacked(qkv[r, lanes(quad * QUAD, QUAD)], masks)
        scores = nt(q, qkv[r, lanes(width + quad * QUAD, QUAD)]) * HD ** -0.5
        e = jnp.exp(scores - jnp.max(scores, -1, keepdims=True))
        p = e / jnp.sum(e, -1, keepdims=True)
        p = p.astype(BF16)
        probs[n] = p
        o = nn(p, qkv[r, lanes(2 * width + quad * QUAD, QUAD)])
        att[r, lanes(quad * QUAD, QUAD)] = picked(o, masks).astype(BF16)
        return c
    lax.fori_loop(0, 3 * segs, attend, 0)
    save(probs, probs_o); save(att, att_o)
    loads[1].wait()
    acc[...] = nn(att[...], wproj[...])
    def first(n, c):
        r = pl.ds(pl.multiple_of(n * length, length), length)
        u, i = unit(x[r, :].astype(F32) + acc[r, :])
        unit1[r, :] = u
        inv[0, r, :] = jnp.broadcast_to(i, (length, 128))
        f = u * ga
        acc[r, :] = f
        low[r, :] = f.astype(BF16)
        return c
    lax.fori_loop(0, segs, first, 0)
    save(unit1, unit1_o)
    loads[2].wait()
    tile = 512
    def up(n, c):
        s = lanes(n * tile, tile)
        h, g = gelu_pair(nn(low[...], wup[:, s]))
        hidden[:, s] = h.astype(BF16)
        slope[:, s] = g.astype(BF16)
        return c
    lax.fori_loop(0, wup.shape[1] // tile, up, 0)
    save(hidden, hidden_o); save(slope, slope_o)
    loads[3].wait()
    def down(n, c):
        s = lanes(n * QUAD, QUAD)
        acc[:, s] += nn(hidden[...], wdown[:, s])
        return c
    lax.fori_loop(0, width // QUAD, down, 0)
    def second(n, c):
        r = pl.ds(pl.multiple_of(n * length, length), length)
        u, i = unit(acc[r, :])
        unit2[r, :] = u
        inv[1, r, :] = jnp.broadcast_to(i, (length, 128))
        return c
    lax.fori_loop(0, segs, second, 0)
    save(unit2, unit2_o); save(inv, inv_o)
    for copy in saves: copy.wait()

ANY = pl.BlockSpec(memory_space=pl.ANY)
VM = pl.BlockSpec(memory_space=pltpu.VMEM)
def sds(*a): return jax.ShapeDtypeStruct(*a)

def forward(x, segs, weights):
    w_in, w_proj, ga, w_up, w_down = weights[:5]
    rows, width = x.shape
    ff = w_up.shape[1]
    length = rows // segs
    saved = [((rows, 3 * width), BF16), ((3 * segs, 4 * length, length), BF16), ((rows, width), BF16), ((rows, width), F32),
             ((rows, width), F32), ((2, rows, 128), F32), ((rows, ff), BF16), ((rows, ff), BF16)]
    return pl.pallas_call(
        partial(forward_kernel, segs),
        out_shape=[sds(*s) for s in saved],
        in_specs=[VM, ANY, ANY, ANY, ANY, VM],
        out_specs=[ANY] * 8,
        scratch_shapes=[pltpu.VMEM(w.shape, BF16) for w in (w_in, w_proj, w_up, w_down)]
        + [pltpu.VMEM(*s) for s in saved]
        + [pltpu.VMEM((rows, width), F32), pltpu.VMEM((rows, width), BF16), pltpu.SemaphoreType.DMA((4,)), pltpu.SemaphoreType.DMA((8,))],
        compiler_params=pltpu.CompilerParams(vmem_limit_bytes=60 << 20),
        name="segment_forward",
    )(x, w_in, w_proj, w_up, w_down, ga)


def spots():
    dp, seg = lax.axis_index("dp"), lax.axis_index("seg")
    return dp // 2, dp % 2, seg // 2, seg % 2

def norm_back(u, i, up, gain):
    s = up * gain
    return i * (s - mean(s) - u * mean(s * u)), jnp.sum(up * u, 0, keepdims=True)

def exact(a, b, dims=(((1,), (0,)), ((), ()))):
    return lax.dot_general(a, b, dims, precision=lax.Precision.HIGHEST, preferred_element_type=F32)

def row_spots(shape, axis):
    r = lax.broadcasted_iota(jnp.int32, shape, axis)
    core, x, y, z, s = r // 64, r // 32 % 2, r // 16 % 2, r // 4 % 4, r % 4
    return 2 * y + x, s * 8 + 2 * z + core

def row_docs(shape, axis, counts):
    slot, place = row_spots(shape, axis)
    document, begin, first = jnp.zeros(shape, jnp.int32), jnp.zeros(shape, jnp.int32), jnp.zeros(shape, jnp.int32)
    for s in range(counts.shape[0]):
        end = jnp.int32(0)
        for d in range(counts.shape[1]):
            start, end = end, end + counts[s, d]
            here = slot == s
            document += jnp.where(here & (end <= place), 1, 0)
            begin = jnp.where(here & (start <= place) & (place < end), start, begin)
            first = jnp.where(here & (start == place), 1, first)
    return slot, place, document, place - begin, first


def slot_of(chunk):
    return chunk if chunk < GS else (3, 0, 1, 2)[chunk - GS]

class Reducer:
    def __init__(self, g, bufs):
        self.g = g
        self.r1, self.r2, self.r3, self.r4, self.own, self.peer, self.gain, self.ss, self.rs, self.zs, self.zr, self.gs, self.gr = bufs
        self.y, self.x, self.z, self.core = y, x, z, core = spots()
        self.dp, self.seg = lax.axis_index("dp"), lax.axis_index("seg")
        self.xn, self.yn, self.cn = (2 * y + 1 - x, self.seg), (2 * (1 - y) + x, self.seg), (self.dp, 2 * z + 1 - core)
        self.zt = [lax.rem(z + k, 4) for k in (1, 2, 3)]
        self.zn = [(self.dp, 2 * t + core) for t in self.zt]
        self.order = ((x, y, self.xn, self.yn), (y, x, self.yn, self.xn))

    @staticmethod
    def scratch(width):
        dma = pltpu.SemaphoreType.DMA
        v = lambda *s: pltpu.VMEM(s + (48, 384), BF16)
        return [v(NC, 2, 2, 2, 2), v(NC, 2, 2, 2), v(NC, 4), v(NC, 3), v(NC), v(NC), pltpu.VMEM((7, 2, width), F32),
                dma((6, NC)), dma((6, NC)), dma((3, NC)), dma((3, NC)), dma((6,)), dma((6,))]

    def greet(self):
        barrier = pltpu.get_barrier_semaphore()
        for d in [self.xn, self.yn, self.cn] + self.zn:
            pl.semaphore_signal(barrier, inc=1, device_id=d, device_id_type=MESH)
    def met(self):
        pl.semaphore_wait(pltpu.get_barrier_semaphore(), 6)

    def copy(self, src, dst, s, r, to):
        return pltpu.make_async_remote_copy(src, dst, s, r, device_id=to, device_id_type=MESH)
    def s1(self, c):
        return self.copy(self.g.at[slot_of(c), 1 - self.core], self.r1.at[c], self.ss.at[0, c], self.rs.at[0, c], self.cn)
    def s2(self, c, h):
        p, q, pn, qn = self.order[h]
        return self.copy(self.r1.at[c, h, 1 - p], self.r2.at[c, h], self.ss.at[1 + h, c], self.rs.at[1 + h, c], pn)
    def s3(self, c, h):
        p, q, pn, qn = self.order[h]
        return self.copy(self.r2.at[c, h, 1 - q], self.r3.at[c, pl.ds(2 * h, 2)], self.ss.at[3 + h, c], self.rs.at[3 + h, c], qn)
    def s4(self, c, k):
        return self.copy(self.r3.at[c, self.zt[k]], self.r4.at[c, k], self.zs.at[k, c], self.zr.at[k, c], self.zn[k])
    def s5(self, c):
        return self.copy(self.own.at[c], self.peer.at[c], self.ss.at[5, c], self.rs.at[5, c], self.xn)
    def if_needed(self, c, x, act):
        if c in (4, 5, 9):
            pl.when(x == 0)(act)
        elif c in (6, 7, 11):
            pl.when(x == 1)(act)
        else:
            act()

    @staticmethod
    def add(*terms):
        total = terms[0].astype(F32)
        for t in terms[1:]:
            total = total + t.astype(F32)
        return total.astype(BF16)

    def start(self, c):
        self.s1(c).start()
    def core_done(self, c):
        self.s1(c).wait()
        for h in (0, 1):
            p = self.order[h][0]
            for at in (1 - p, p):
                def one(k, carry, h=h, at=at):
                    self.r1[c, h, at, k // 2, k % 2] = self.add(self.g[slot_of(c), self.core, h, at, k // 2, k % 2], self.r1[c, h, at, k // 2, k % 2])
                    return carry
                lax.fori_loop(0, 4, one, 0)
                if at is not p:
                    self.s2(c, h).start()
    def first_done(self, c):
        for h in (0, 1):
            self.s2(c, h).wait()
            def one(k, carry, h=h):
                self.r2[c, h, k // 2, k % 2] = self.add(self.r1[c, h, self.order[h][0], k // 2, k % 2], self.r2[c, h, k // 2, k % 2])
                return carry
            lax.fori_loop(0, 4, one, 0)
            self.s3(c, h).start()
    def second_done(self, c):
        for h in (0, 1):
            self.s3(c, h).wait()
            for zz in (0, 1):
                self.r3[c, 2 * h + zz] = self.add(self.r2[c, h, self.order[h][1], zz], self.r3[c, 2 * h + zz])
        for k in range(3): self.s4(c, k).start()
    def line_done(self, c):
        for k in range(3): self.s4(c, k).wait()
        self.own[c] = self.add(self.r3[c, self.z], self.r4[c, 0], self.r4[c, 1], self.r4[c, 2])
        self.if_needed(c, 1 - self.x, lambda: self.s5(c).start())
    def swap_done(self, c):
        self.if_needed(c, 1 - self.x, lambda: self.s5(c).wait_send())
        self.if_needed(c, self.x, lambda: self.s5(c).wait_recv())

    def gain_copies(self, stage):
        if stage < 3:
            to = (self.cn, self.xn, self.yn)[stage]
            return [self.copy(self.gain.at[0], self.gain.at[1 + stage], self.gs.at[stage], self.gr.at[stage], to)]
        return [self.copy(self.gain.at[0], self.gain.at[4 + k], self.gs.at[3 + k], self.gr.at[3 + k], self.zn[k]) for k in range(3)]
    def gain_start(self, stage):
        for c in self.gain_copies(stage): c.start()
    def gain_done(self, stage):
        for c in self.gain_copies(stage): c.wait()
        if stage < 3:
            self.gain[0] = self.gain[0] + self.gain[1 + stage]
        else:
            self.gain[0] = self.gain[0] + self.gain[4] + self.gain[5] + self.gain[6]


class Pipeline:
    def __init__(self, red):
        self.red, self.flying = red, []
    def move(self, *new):
        r = self.red
        for c in new:
            r.start(c)
        acts = (r.core_done, r.first_done, r.second_done, r.line_done, r.swap_done)
        for k, (c, stage) in enumerate(self.flying):
            acts[stage](c)
            self.flying[k] = (c, stage + 1)
        self.flying = [f for f in self.flying if f[1] < 5] + [(c, 0) for c in new]

def finish_kernel(segs, x_h, cot_h, counts, pads, embed, w_in, w_proj, w_up, w_down, ga_v, gf_v, cw_in, cw_proj, cw_up, cw_down, cga_v, cgf_v, *rest):
    saved_h, rest = rest[:8], rest[8:]
    token_o, out_o, own_o, peer_o, d_up0, d_down0, c_in, c_proj, c_up, c_down, small_o, embed_o = rest[:12]
    cot, win, wproj, wup, wdown, qkv, probs, att, unit1, unit2, inv, hidden, slope, low, dy, outb, g, pay, buf, slope0, base, cross_cot, gains = rest[12:35]
    in_sem, again_sem, out_sem, local, gs, gr = rest[35:41]
    red = Reducer(g, rest[41:])
    pipe = Pipeline(red)
    y, x_at, z, core = red.y, red.x, red.z, red.core
    rows, width = x_h.shape
    length = rows // segs
    ff = wup.shape[1]
    ga, gf, cga, cgf = row(ga_v), row(gf_v), row(cga_v), row(cgf_v)
    tile = 512

    names = ("cot", "unit2", "inv", "unit1", "hidden", "wdown", "slope", "wup", "cwin", "cwproj", "att", "qkv", "probs")
    pairs = ((cot_h, cot), (saved_h[4], unit2), (saved_h[5], inv), (saved_h[3], unit1), (saved_h[6], hidden), (w_down, wdown), (saved_h[7], slope),
             (w_up, wup), (cw_in, win), (cw_proj, wproj), (saved_h[2], att), (saved_h[0], qkv), (saved_h[1], probs))
    loads = {k: pltpu.make_async_copy(a, b, in_sem.at[n]) for n, (k, (a, b)) in enumerate(zip(names, pairs))}
    for load in loads.values(): load.start()
    again = {}
    def reload(name, src, dst):
        again[name] = pltpu.make_async_copy(src, dst, again_sem.at[len(again)])
        again[name].start()
    red.greet()

    for k in ("cot", "unit2", "inv", "unit1"): loads[k].wait()
    for s in range(segs):
        r = slice(s * length, s * length + 1)
        pay[s : s + 1, :width] = unit1[r, :]
        pay[s : s + 1, width : 2 * width] = unit2[r, :]
        pay[s : s + 1, 2 * width : 3 * width] = cot[s * length : s * length + 16, :].astype(F32)[:1]
        pay[s : s + 1, 3 * width :] = inv[1, r, :]
    top = lax.broadcasted_iota(jnp.int32, (length, 1), 0) == 0
    gains[...] = jnp.zeros_like(gains)
    def second(n, c):
        r = pl.ds(pl.multiple_of(n * length, length), length)
        up = jnp.where(top, 0.0, cot[r, :].astype(F32))
        u = unit2[r, :]
        outb[r, :] = (u * gf).astype(BF16)
        d, gain = norm_back(u, inv[1, r, :1], up, gf)
        gains[1:2, :] += gain
        unit2[r, :] = d
        dy[r, :] = d.astype(BF16)
        low[r, :] = (unit1[r, :] * ga).astype(BF16)
        return c
    lax.fori_loop(0, segs, second, 0)

    red.met()
    mine = buf.at[core, x_at, y, z]
    keep = pltpu.make_async_copy(pay, mine, local.at[0])
    keep.start()
    send = lambda src, dst, k, to: red.copy(src, dst, gs.at[k], gr.at[k], to)
    along_z = [send(pay, mine, k, red.zn[k]) for k in range(3)]
    later = [send(p, p, k, to) for k, p, to in ((3, buf.at[core, x_at, y], red.yn), (4, buf.at[core, x_at], red.xn), (5, buf.at[core], red.cn))]
    for s in along_z: s.start()

    loads["hidden"].wait()
    def down_grad(j, c):
        v = tn(hidden[:, lanes(j * 384, 384)], dy[...]).astype(BF16)
        z_to, core_to = j // 2, j % 2
        h, zz = z_to // 2, z_to % 2
        for chunk in range(4):
            for half in range(2):
                for side in range(2):
                    part = v[chunk * 96 + half * 48 : chunk * 96 + half * 48 + 48, side * 384 : side * 384 + 384]
                    g[chunk, core_to, h, half * (1 - h) + side * h, side * (1 - h) + half * h, zz] = part
        return c
    lax.fori_loop(0, 4, down_grad, 0)
    keep.wait()
    for s in along_z: s.wait()
    later[0].start()
    lax.fori_loop(4, 8, down_grad, 0)
    pipe.move(0)
    later[0].wait(); later[1].start()

    loads["slope"].wait()
    for s in range(segs):
        slope0[s : s + 1, :] = slope[s * length : s * length + 16, :].astype(F32)[:1]
    loads["wdown"].wait()
    def pre_grad(n, c):
        s = lanes(n * tile, tile)
        slope[:, s] = (nt(dy[...], wdown[pl.ds(pl.multiple_of(n * tile, tile), tile), :]) * slope[:, s].astype(F32)).astype(BF16)
        return c
    lax.fori_loop(0, 3, pre_grad, 0)
    pipe.move(1)
    lax.fori_loop(3, ff // tile, pre_grad, 0)
    later[1].wait(); later[2].start()
    reload("cwdown", cw_down, wdown)
    pipe.move(2)

    def put(slot, side, v):
        v = v.astype(BF16)
        for j in range(8):
            z_to, core_to = j // 2, j % 2
            h, zz = z_to // 2, z_to % 2
            for half in range(2):
                p, q = (half, side) if h == 0 else (side, half)
                g[slot, core_to, h, p, q, zz] = v[j * 96 + half * 48 : j * 96 + half * 48 + 48]
    def up_grad(n, c):
        chunk, side = n // 2, n % 2
        put(4 + chunk, side, tn(low[...], slope[:, lanes(side * (ff // 2) + chunk * 384, 384)]))
        return c
    lax.fori_loop(0, 8, up_grad, 0)
    reload("x", x_h, low)
    pipe.move(3)
    loads["wup"].wait()
    def first_grad(n, c):
        unit2[:, lanes(n * QUAD, QUAD)] += nt(slope[...], wup[pl.ds(pl.multiple_of(n * QUAD, QUAD), QUAD), :])
        return c
    lax.fori_loop(0, width // QUAD, first_grad, 0)
    reload("cwup", cw_up, wup)
    later[2].wait()
    pipe.move(4)

    n = 128
    unit1_all = jnp.concatenate([buf[k // 16, k // 8 % 2, k // 4 % 2, k % 4, :, :width] for k in range(32)], 0)
    unit2_all = jnp.concatenate([buf[k // 16, k // 8 % 2, k // 4 % 2, k % 4, :, width : 2 * width] for k in range(32)], 0)
    base[0] = unit1_all
    base[1] = unit2_all
    cross_cot[...] = jnp.concatenate([buf[k // 16, k // 8 % 2, k // 4 % 2, k % 4, :, 2 * width : 3 * width] for k in range(32)], 0)
    inv_all = jnp.concatenate([buf[k // 16, k // 8 % 2, k // 4 % 2, k % 4, :, 3 * width :] for k in range(32)], 0)[:, :1]
    slot_c, place_c, doc_c, rank_c, first_c = row_docs((n, 1), 0, counts)
    slot_r, place_r, doc_r, rank_r, first_r = row_docs((1, n), 1, counts)
    places = lax.broadcasted_iota(jnp.int32, (32, n), 0)
    by_slot = exact(pads[...].astype(F32), (places == place_r).astype(F32))
    pad_r = jnp.zeros((1, n), F32)
    for s in range(pads.shape[0]):
        pad_r = jnp.where(slot_r == s, by_slot[s : s + 1], pad_r)
    allowed = (slot_c == slot_r) & (doc_c == doc_r) & ((pad_r == 0) | (first_r == 1))
    pick = (rank_c == lax.broadcasted_iota(jnp.int32, (n, 32), 1)).astype(F32)
    xin = base[1] * gf + exact(pick, embed[...])
    xl = xin.astype(BF16)
    masks = head_mask(n)
    wide = jnp.concatenate([allowed.astype(F32)] * 4, 0) > 0
    loads["cwin"].wait()
    cqkv = jnp.concatenate([nn(xl, win[:, k * width : (k + 1) * width]).astype(BF16) for k in range(3)], 1)
    cprobs, catts = [], []
    part = lambda a, k, quad: a[:, k * width + quad * QUAD : k * width + quad * QUAD + QUAD]
    for quad in range(3):
        scores = jnp.where(wide, nt(stacked(part(cqkv, 0, quad), masks), part(cqkv, 1, quad)) * HD ** -0.5, MASKED)
        e = jnp.exp(scores - jnp.max(scores, -1, keepdims=True))
        p = e / jnp.sum(e, -1, keepdims=True)
        cprobs.append(p)
        catts.append(picked(nn(p.astype(BF16), part(cqkv, 2, quad)), masks).astype(BF16))
    catt = jnp.concatenate(catts, 1)
    loads["cwproj"].wait()
    u1, i1 = unit(xin + nn(catt, wproj[...]))
    f = u1 * cga
    fl = f.astype(BF16)
    pipe.move(5)
    hid, dpre, slp = slice(0, n), slice(n, 2 * n), slice(2 * n, 3 * n)
    again["cwup"].wait()
    def up(k, c):
        s = lanes(k * tile, tile)
        h, gl = gelu_pair(nn(fl, wup[:, s]))
        hidden[hid, s] = h.astype(BF16)
        hidden[slp, s] = gl.astype(BF16)
        return c
    lax.fori_loop(0, ff // tile, up, 0)
    again["cwdown"].wait()
    u2, i2 = unit(f + nn(hidden[hid, :], wdown[...]))
    me = ((core * 2 + x_at) * 2 + y) * 4 + z
    own = (lax.broadcasted_iota(jnp.int32, (8, n), 1) == 4 * me + lax.broadcasted_iota(jnp.int32, (8, n), 0)).astype(F32)
    result = exact(own, u2 * cgf)
    for s in range(segs):
        r = slice(s * length, s * length + 16)
        outb[r, :] = jnp.where(top[:16], result[s : s + 1], outb[r, :].astype(F32)).astype(BF16)
    saves = [pltpu.make_async_copy(outb, out_o, out_sem.at[0])]
    saves[0].start()
    d2, cgain_f = norm_back(u2, i2, cross_cot[...], cgf)
    dy2 = d2.astype(BF16)
    pipe.move(6)
    def pre(k, c):
        s = lanes(k * tile, tile)
        hidden[dpre, s] = (nt(dy2, wdown[pl.ds(pl.multiple_of(k * tile, tile), tile), :]) * hidden[slp, s].astype(F32)).astype(BF16)
        return c
    lax.fori_loop(0, ff // tile, pre, 0)
    reload("wdown", w_down, wdown)
    d1, cgain_a = norm_back(u1, i1, d2 + nt(hidden[dpre, :], wup[...]), cga)
    reload("wup", w_up, wup)
    dy1 = d1.astype(BF16)
    datt = nt(dy1, wproj[...]).astype(BF16)
    reload("wproj", w_proj, wproj)
    dq, dk, dv = [], [], []
    for quad in range(3):
        da = stacked(part(datt, 0, quad), masks)
        q, k = stacked(part(cqkv, 0, quad), masks), part(cqkv, 1, quad)
        p = cprobs[quad]
        dp = nt(da, part(cqkv, 2, quad))
        ds = (p * (dp - jnp.sum(p * dp, -1, keepdims=True))).astype(BF16)
        dq.append((picked(nn(ds, k), masks) * HD ** -0.5).astype(BF16))
        dk.append((tn(ds, q) * HD ** -0.5).astype(BF16))
        dv.append(tn(p.astype(BF16), da).astype(BF16))
    dqkv = jnp.concatenate(dq + dk + dv, 1)
    crossed = d1 + nt(dqkv, win[...])
    reload("win", w_in, win)
    pipe.move(7)

    unit2_0 = base[1]
    d20, spare = norm_back(unit2_0, inv_all, crossed, gf)
    mine_up, mine_d2 = exact(own, crossed), exact(own, d20)
    gains[1:2, :] += jnp.sum((mine_up * exact(own, unit2_0))[:segs], 0, keepdims=True)
    dy0 = d20.astype(BF16)
    mine_dy = mine_d2.astype(BF16)
    f0 = (base[0] * ga).astype(BF16)
    i, j = 2 * y + x_at, 2 * z + core
    def turn(a, by):
        a = a.astype(F32)
        return pltpu.roll(a, lax.rem(a.shape[1] - by, a.shape[1]), 1).astype(BF16)
    sixth = width // 8
    left = lambda a: turn(a, sixth * j)[:, :128]
    again["wdown"].wait()
    again["wup"].wait()
    quarter, eighth = ff // 4, ff // 8
    hid0, spare = gelu_pair(nn(f0, wup[:, lanes(eighth * j, eighth)]))
    d_down0[...] = tn(hid0.astype(BF16), turn(dy0, width // 4 * i)[:, :256])[:, : width // 4]
    spare, slope_0 = gelu_pair(nn(f0, wup[:, lanes(quarter * i, quarter)]))
    du0 = (nt(dy0, wdown[pl.ds(pl.multiple_of(quarter * i, quarter), quarter), :]) * slope_0).astype(BF16)
    d_up0[...] = tn(left(f0), du0)[:sixth]
    def mine_pre(k, d):
        s = lanes(k * tile, tile)
        du = (nt(mine_dy, wdown[pl.ds(pl.multiple_of(k * tile, tile), tile), :]) * slope0[:, s]).astype(BF16)
        return d + nt(du, wup[:, s])
    mine_first = lax.fori_loop(0, ff // tile, mine_pre, mine_d2)
    for s in range(segs):
        unit2[s * length : s * length + 1, :] = mine_first[s : s + 1]

    def first(k, c):
        r = pl.ds(pl.multiple_of(k * length, length), length)
        d, gain = norm_back(unit1[r, :], inv[0, r, :1], unit2[r, :], ga)
        gains[0:1, :] += gain
        unit1[r, :] = d
        dy[r, :] = d.astype(BF16)
        return c
    lax.fori_loop(0, segs, first, 0)
    red.gain[0] = gains[...]
    loads["att"].wait()
    def proj_grad(side, c):
        put(slot_of(8), side, tn(att[...], dy[:, lanes(side * 384, 384)]))
        return c
    lax.fori_loop(0, 2, proj_grad, 0)
    pipe.move(8)
    red.gain_start(0)
    again["wproj"].wait()
    att[...] = nt(dy[...], wproj[...]).astype(BF16)
    loads["qkv"].wait()
    loads["probs"].wait()
    def attend(k, c):
        seg, quad = k // 3, k % 3
        r = pl.ds(pl.multiple_of(seg * length, length), length)
        qs, ks, vs = (lanes(m * width + quad * QUAD, QUAD) for m in range(3))
        da = stacked(att[r, lanes(quad * QUAD, QUAD)], masks)
        q, keys = stacked(qkv[r, qs], masks), qkv[r, ks]
        plow = probs[k]
        p = plow.astype(F32)
        dp = nt(da, qkv[r, vs])
        ds = (p * (dp - jnp.sum(p * dp, -1, keepdims=True))).astype(BF16)
        qkv[r, qs] = (picked(nn(ds, keys), masks) * HD ** -0.5).astype(BF16)
        qkv[r, ks] = (tn(ds, q) * HD ** -0.5).astype(BF16)
        qkv[r, vs] = tn(plow, da).astype(BF16)
        return c
    lax.fori_loop(0, 6, attend, 0)
    red.gain_done(0); red.gain_start(1)
    pipe.move()
    lax.fori_loop(6, 3 * segs, attend, 0)
    red.gain_done(1); red.gain_start(2)
    again["x"].wait()
    for chunk in range(3):
        def in_grad(side, c):
            put(slot_of(9 + chunk), side, tn(low[...], qkv[:, lanes(side * (3 * width // 2) + chunk * 384, 384)]))
            return c
        lax.fori_loop(0, 2, in_grad, 0)
        pipe.move(9 + chunk)
    red.gain_done(2); red.gain_start(3)
    again["win"].wait()
    def token(k, c):
        s = lanes(k * QUAD, QUAD)
        cot[:, s] = (unit1[:, s] + nt(qkv[...], win[pl.ds(pl.multiple_of(k * QUAD, QUAD), QUAD), :])).astype(BF16)
        return c
    lax.fori_loop(0, width // QUAD, token, 0)
    saves.append(pltpu.make_async_copy(cot, token_o, out_sem.at[1]))
    saves[1].start()
    pipe.move()
    c_in[...] = tn(left(xl), turn(dqkv, 3 * width // 4 * i)[:, :640])[:sixth, : 3 * width // 4]
    c_proj[...] = tn(left(catt), turn(dy1, width // 4 * i)[:, :256])[:sixth, : width // 4]
    c_up[...] = tn(left(fl), hidden[dpre, lanes(quarter * i, quarter)])[:sixth]
    c_down[...] = tn(hidden[hid, lanes(eighth * j, eighth)], turn(dy2, width // 4 * i)[:, :256])[:, : width // 4]
    pick8 = (rank_c - 8 * i == lax.broadcasted_iota(jnp.int32, (n, 8), 1)).astype(F32)
    by_rank = exact(pick8, crossed, (((0,), (0,)), ((), ())))
    embed_o[...] = pltpu.roll(by_rank, lax.rem(width - sixth * j, width), 1)[:, :sixth]
    pipe.move()
    red.gain_done(3)
    every = jnp.concatenate([red.gain[0], cgain_a, cgain_f, jnp.zeros((4, width), F32)], 0)
    small_o[...] = pltpu.roll(every, lax.rem(width - sixth * j, width), 1)[:, :128]
    while pipe.flying:
        pipe.move()
    saves += [pltpu.make_async_copy(red.own, own_o, out_sem.at[2]), pltpu.make_async_copy(red.peer, peer_o, out_sem.at[3])]
    for s in saves[2:]: s.start()
    for s in saves: s.wait()

def finish(x, cot, counts, pads, embed, saved, segs, weights, cross_weights):
    w_in, w_proj, ga, w_up, w_down, gf = weights
    cw_in, cw_proj, cga, cw_up, cw_down, cgf = cross_weights
    rows, width = x.shape
    ff = w_up.shape[1]
    sixth = width // 8
    outs = [((rows, width), BF16)] * 2 + [((NC, 48, 384), BF16)] * 2 + [((sixth, ff // 4), F32), ((ff // 8, width // 4), F32),
            ((sixth, 3 * width // 4), F32), ((sixth, width // 4), F32), ((sixth, ff // 4), F32), ((ff // 8, width // 4), F32),
            ((8, 128), F32), ((8, sixth), F32)]
    dma = pltpu.SemaphoreType.DMA
    v = lambda *s: pltpu.VMEM(s, BF16)
    return pl.pallas_call(
        partial(finish_kernel, segs), out_shape=[sds(*o) for o in outs],
        in_specs=[ANY, ANY, pl.BlockSpec(memory_space=pltpu.SMEM), VM, VM, ANY, ANY, ANY, ANY, VM, VM, ANY, ANY, ANY, ANY, VM, VM] + [ANY] * 8,
        out_specs=[ANY] * 4 + [VM] * 8,
        scratch_shapes=[v(rows, width)] + [pltpu.VMEM(w.shape, BF16) for w in (w_in, w_proj, w_up, w_down)]
        + [pltpu.VMEM(s.shape, s.dtype) for s in saved]
        + [v(rows, width)] * 3 + [v(GS, 2, 2, 2, 2, 2, 48, 384), pltpu.VMEM((segs, PAY), F32), pltpu.VMEM((2, 2, 2, 4, segs, PAY), F32),
           pltpu.VMEM((8, ff), F32), pltpu.VMEM((2, 128, width), F32), pltpu.VMEM((128, width), F32), pltpu.VMEM((2, width), F32),
           dma((13,)), dma((7,)), dma((4,)), dma((1,)), dma((6,)), dma((6,))]
        + Reducer.scratch(width),
        compiler_params=pltpu.CompilerParams(collective_id=0, has_side_effects=True, vmem_limit_bytes=67043328), name="finish",
    )(x, cot, counts, pads, embed, w_in, w_proj, w_up, w_down, ga, gf, cw_in, cw_proj, cw_up, cw_down, cga, cgf, *saved)

def deliver_kernel(own, peer, d_up0, d_down0, small, token_i, out_i, ci_in, ci_proj, ci_up, ci_down, ci_embed,
                   d_in, d_proj, d_up, d_down, g0, g1, g2, g3, token_o, out_o, c_in, c_proj, c_up, c_down, embed_o, token, out, sem):
    big = [(token_i, token, token_o), (out_i, out, out_o)]
    loads = [pltpu.make_async_copy(a, b, sem.at[k]) for k, (a, b, c) in enumerate(big)]
    stores = [pltpu.make_async_copy(b, c, sem.at[2 + k]) for k, (a, b, c) in enumerate(big)]
    for load in loads: load.start()
    at = lax.rem(lax.axis_index("dp"), 2)
    for mine in (0, 1):
        @pl.when(at == mine)
        def _():
            for half in (0, 1):
                a = own if half == mine else peer
                r = slice(48 * half, 48 * half + 48)
                side = slice(192 * mine, 192 * mine + 192)
                d_proj[r, :] = a[8, :, side].astype(F32)
                for k in range(2):
                    s = slice(384 * k, 384 * k + 384)
                    d_up[r, s] = a[4 + 2 * mine + k].astype(F32) + d_up0[r, s]
                parts = [a[9], a[10, :, side]] if mine == 0 else [a[10, :, side], a[11]]
                d_in[r, :] = jnp.concatenate(parts, 1).astype(F32)
                for k in range(4):
                    s = slice(96 * k + 48 * half, 96 * k + 48 * half + 48)
                    d_down[s, :] = a[k, :, side].astype(F32) + d_down0[s, :]
    for load, store in zip(loads, stores):
        load.wait(); store.start()
    for k, o in enumerate((g0, g1, g2, g3)):
        o[...] = small[k : k + 1, : o.shape[0]].reshape(o.shape)
    for a, b in ((ci_in, c_in), (ci_proj, c_proj), (ci_up, c_up), (ci_down, c_down), (ci_embed, embed_o)):
        b[...] = a[...]
    for store in stores: store.wait()

def deliver(token, out, own, peer, d_up0, d_down0, c_in, c_proj, c_up, c_down, small, embed):
    width = token.shape[1]
    sixth = width // 8
    like = lambda a: sds(a.shape, a.dtype)
    outs = [sds((sixth, 3 * width // 4), F32), sds((sixth, width // 4), F32), like(d_up0), like(d_down0)] + [sds((sixth,), F32)] * 4 + [
        like(a) for a in (token, out, c_in, c_proj, c_up, c_down, embed)]
    return pl.pallas_call(
        deliver_kernel, out_shape=outs, in_specs=[VM] * 5 + [ANY, ANY] + [VM] * 5, out_specs=[VM] * 8 + [ANY, ANY] + [VM] * 5,
        scratch_shapes=[pltpu.VMEM(token.shape, BF16)] * 2 + [pltpu.SemaphoreType.DMA((4,))],
        compiler_params=pltpu.CompilerParams(vmem_limit_bytes=20 << 20), name="deliver",
    )(own, peer, d_up0, d_down0, small, token, out, c_in, c_proj, c_up, c_down, embed)


def this_mesh(
    tokens, doc_counts, pad_mask, attn_in, attn_proj, norm_attn, ffn_up, ffn_down, norm_ffn,
    segment_embed, cross_in, cross_proj, cross_norm_attn, cross_up, cross_down, cross_norm_ffn,
    cotangent,
):
    segs, length, width = tokens.shape
    x, cot = tokens.reshape(segs * length, width), cotangent.reshape(segs * length, width)
    weights = (attn_in, attn_proj, norm_attn, ffn_up, ffn_down, norm_ffn)
    cross_weights = (cross_in, cross_proj, cross_norm_attn, cross_up, cross_down, cross_norm_ffn)
    saved = forward(x, segs, weights)
    done = finish(x, cot, doc_counts, pad_mask, segment_embed, saved, segs, weights, cross_weights)
    d_in, d_proj, d_up, d_down, n_attn, n_ffn, c_attn, c_ffn, token, out, c_in, c_proj, c_up, c_down, embed = deliver(*done)
    return (
        out.reshape(tokens.shape), token.reshape(tokens.shape), d_in, d_proj, n_attn, d_up, d_down, n_ffn,
        embed, c_in, c_proj, c_attn, c_up, c_down, c_ffn,
    )


def solution(mesh):
    fits = (mesh.shape["dp"], mesh.shape["seg"]) == (4, 8)
    placed = (
        P(("dp", "seg"), None, None),
        P(),
        P(),
        P(),
        P(),
        P(),
        P(),
        P(),
        P(),
        P(),
        P(),
        P(),
        P(),
        P(),
        P(),
        P(),
        P(("dp", "seg"), None, None),
    )
    return jax.shard_map(
        this_mesh if fits else any_mesh,
        mesh=mesh,
        in_specs=placed,
        out_specs=(
            P(("dp", "seg"), None, None),
            P(("dp", "seg"), None, None),
            P("seg", "dp"),
            P("seg", "dp"),
            P("seg"),
            P("seg", "dp"),
            P("seg", "dp"),
            P("seg"),
            P("dp", "seg"),
            P("seg", "dp"),
            P("seg", "dp"),
            P("seg"),
            P("seg", "dp"),
            P("seg", "dp"),
            P("seg"),
        ),
        check_vma=False,
    )
```
